32 devices in a mesh: wide: 16 (over z, x, core), narrow: 2 (over y).
Axes of the slice: x: 2, y: 2, z: 4, core: 2. Of those that a mesh axis runs over, the one named last changes fastest.
Arguments:
- edge_msg: bfloat16 [8192, 1024], P(('wide', 'narrow')), may hold values from -6 to 6
- basis: bfloat16 [8192, 512], P(('wide', 'narrow')), may hold values from -1.5 to 1.5
- atom_h: bfloat16 [1024, 512], P('narrow'), may hold values from -6 to 6
- edge_source: int32 [8192], P(('wide', 'narrow')), may hold values from 0 to 1023
- edge_target: int32 [8192], P(('wide', 'narrow')), may hold values from 0 to 1023, as said below
- send_rows: int32 [32, 512], P(('wide', 'narrow')), may hold values from 0 to 255
- trip_slot: int32 [8192, 32], P(('wide', 'narrow')), may hold values from 0 to 511, as said below
- w_down: bfloat16 [1024, 64], replicated, may hold values from -0.1875 to 0.1875
- w_bil: bfloat16 [1024, 64], replicated, may hold values from -0.1875 to 0.1875
- w_up: bfloat16 [64, 1024], replicated, may hold values from -0.75 to 0.75
- w_atom_in: bfloat16 [1024, 512], replicated, may hold values from -0.1875 to 0.1875
- atom_gain: float32 [512], replicated, may hold values from 0.5 to 1.5
- w_atom: bfloat16 [512, 512], replicated, may hold values from -0.25 to 0.25
- w_src: bfloat16 [512, 1024], replicated, may hold values from -0.25 to 0.25
- w_tgt: bfloat16 [512, 1024], replicated, may hold values from -0.25 to 0.25
Outputs:
- edge_out: bfloat16 [8192, 1024], P(('wide', 'narrow'))
- atom_out: bfloat16 [1024, 512], P('narrow')
The draws below stay inside these ranges and needn't reach their ends.
Inputs may be any that keep to these rules, and one draw needn't show every extreme that they name: `edge_target`: the edges of block b target atoms of the narrow block b % 2, that is (b % 2) * 512 to (b % 2 + 1) * 512 - 1, never outside that range, and never falling (sorted) within a block. `trip_slot`: for each receiving block and each wide index p, the slots p * 32 + c that its triplets use form a prefix c < count of 1 to 32 entries; every block has some p with all 32 used.
All inputs are finite; a program needn't handle non-finite values.
Results may differ from the reference program's by a relative error of at most 0.0065.
Values may be sent and summed in bfloat16 or wider, within the bound.
No kernel may reach another device: no remote copies, remote signals or barrier semaphores. Data moves between devices by JAX's collectives and lax.ppermute only.
A program may use at most 64 MiB of HBM per device.

```python
import jax
import jax.numpy as jnp
from jax import lax

DE = 1024
DT = 64
NB = 16
DA = 512
TRIP = 32
CAP = 32
EDEV = 256
ADEV = 512
EDGES = 8192
ATOMS = 1024
N_WIDE = 16
N_NARROW = 2
DEVICES = 32


def draw_edge_target(key, part):
    blocks = N_WIDE * N_NARROW
    lowest = jnp.arange(blocks, dtype=jnp.int32) % N_NARROW * ADEV
    picks = jax.random.randint(jax.random.fold_in(key, 11), (blocks, EDEV), 0, ADEV, dtype=jnp.int32)
    picks = jnp.sort(picks, axis=1) + lowest[:, None]
    return picks.reshape(-1).astype(jnp.int32)


def draw_trip_slot(key, part):
    blocks = N_WIDE * N_NARROW
    counts = jax.random.randint(jax.random.fold_in(key, 21), (blocks, N_WIDE), 1, CAP + 1, dtype=jnp.int32)
    hottest = jax.random.randint(jax.random.fold_in(key, 22), (blocks, 1), 0, N_WIDE, dtype=jnp.int32)
    counts = jnp.where(jnp.arange(N_WIDE, dtype=jnp.int32)[None, :] == hottest, CAP, counts)
    totals = jnp.cumsum(counts, axis=1).astype(jnp.int32)
    picks = jax.random.randint(jax.random.fold_in(key, 23), (blocks, EDEV * TRIP), 0, totals[:, -1:], dtype=jnp.int32)
    owner = jax.vmap(lambda edges, values: jnp.searchsorted(edges, values, side='right'))(totals, picks).astype(jnp.int32)
    starts = jnp.take_along_axis(totals - counts, owner, axis=1)
    slots = owner * CAP + (picks - starts)
    return slots.reshape(EDGES, TRIP).astype(jnp.int32)


def plant(array, key, low, top_value):
    shape = array.shape
    place = [jax.random.randint(jax.random.fold_in(key, axis), (), 0, shape[axis]) for axis in range(len(shape))]
    array = array.at[tuple(place)].set(low)
    longest = shape.index(max(shape))
    place[longest] = (place[longest] + 1) % shape[longest]
    return array.at[tuple(place)].set(top_value)


def block_scale(key, shape, shards, smallest, largest):
    loudness, own = 1.0, jax.random.fold_in(key, 6)
    for position, parts in shards:
        heights = jnp.exp(jax.random.uniform(jax.random.fold_in(own, position), (parts,), jnp.float32, smallest / len(shards), largest / len(shards)))
        loudness = loudness * jnp.repeat(heights, shape[position] // parts).reshape([-1 if axis == position else 1 for axis in range(len(shape))])
    return loudness


def bell_draw(key, shape, spread, bound, split=(), held_as=jnp.bfloat16):
    values = jax.random.normal(key, shape, jnp.float32) * spread
    if len(split) > 0:
        values = block_scale(key, shape, split, -0.22, 0.18) * values
    return jnp.clip(values, min=-bound, max=bound).astype(held_as)


def setup_inputs(seed: int = 0) -> dict:
    seeds = jax.random.split(jax.random.key(seed), 16)
    return {
        "edge_msg": bell_draw(seeds[0], (EDGES, DE), 1.0, 6.0, ((0, 32),)),
        "basis": bell_draw(seeds[1], (EDGES, TRIP * NB), 0.25, 1.5, ((0, 32),)),
        "atom_h": bell_draw(seeds[2], (ATOMS, DA), 1.0, 6.0, ((0, 2),)),
        "edge_source": plant(jax.random.randint(seeds[3], (EDGES,), 0, ATOMS), jax.random.fold_in(seeds[3], 1), 0, ATOMS - 1).astype(jnp.int32),
        "edge_target": draw_edge_target(jax.random.fold_in(seeds[15], 71), 0),
        "send_rows": plant(jax.random.randint(seeds[5], (DEVICES, N_WIDE * CAP), 0, EDEV), jax.random.fold_in(seeds[5], 1), 0, EDEV - 1).astype(jnp.int32),
        "trip_slot": draw_trip_slot(jax.random.fold_in(seeds[15], 71), 0),
        "w_down": bell_draw(seeds[7], (DE, DT), DE ** -0.5, 0.1875),
        "w_bil": bell_draw(seeds[8], (NB * DT, DT), (NB * DT) ** -0.5, 0.1875),
        "w_up": bell_draw(seeds[9], (DT, DE), DT ** -0.5, 0.75),
        "w_atom_in": bell_draw(seeds[10], (DE, DA), DE ** -0.5, 0.1875),
        "atom_gain": jnp.clip(1.0 + 0.1 * jax.random.normal(seeds[11], (DA,), jnp.float32), 0.5, 1.5),
        "w_atom": bell_draw(seeds[12], (DA, DA), DA ** -0.5, 0.25),
        "w_src": bell_draw(seeds[13], (DA, DE), DA ** -0.5, 0.25),
        "w_tgt": bell_draw(seeds[14], (DA, DE), DA ** -0.5, 0.25),
    }


def silu(value):
    return value / (1.0 + jnp.exp(-value))

def reference(edge_msg, basis, atom_h, edge_source, edge_target, send_rows, trip_slot, w_down, w_bil, w_up, w_atom_in, atom_gain, w_atom, w_src, w_tgt):
    blocks = N_WIDE * N_NARROW
    down = silu(jnp.dot(edge_msg, w_down, preferred_element_type=jnp.float32)).astype(jnp.bfloat16)

    def mix_block(inputs):
        slots, values, block = inputs
        receiver_wide = block // N_NARROW
        narrow_index = block % N_NARROW
        sender = slots // CAP * N_NARROW + narrow_index
        local_edge = send_rows[sender, receiver_wide * CAP + slots % CAP]
        edge_ids = (sender * EDEV + local_edge).astype(jnp.int32)
        other = down[edge_ids].astype(jnp.float32)
        weights = values.reshape(EDEV, TRIP, NB).astype(jnp.float32)
        mixed = jnp.einsum('etk,etc->ekc', weights, other)
        return mixed.reshape(EDEV, NB * DT).astype(jnp.bfloat16)
    mixed = lax.map(mix_block, (trip_slot.reshape(blocks, EDEV, TRIP), basis.reshape(blocks, EDEV, TRIP * NB), jnp.arange(blocks, dtype=jnp.int32)))
    mixed = mixed.reshape(EDGES, NB * DT)
    trip = silu(jnp.dot(mixed, w_bil, preferred_element_type=jnp.float32)).astype(jnp.bfloat16)
    edge_mid = (edge_msg.astype(jnp.float32) + jnp.dot(trip, w_up, preferred_element_type=jnp.float32)).astype(jnp.bfloat16)
    message = jnp.dot(edge_mid, w_atom_in, preferred_element_type=jnp.float32).astype(jnp.bfloat16)
    atom_sum = jax.ops.segment_sum(message.astype(jnp.float32), edge_target, num_segments=ATOMS)
    scale = lax.rsqrt(lax.optimization_barrier(jnp.mean(atom_sum * atom_sum, axis=-1, keepdims=True)) + 1e-06)
    normed = (atom_sum * scale * atom_gain).astype(jnp.bfloat16)
    atom_out = (atom_h.astype(jnp.float32) + silu(jnp.dot(normed, w_atom, preferred_element_type=jnp.float32))).astype(jnp.bfloat16)
    source_rows = atom_out[edge_source]
    target_rows = atom_out[edge_target]
    update = jnp.dot(source_rows, w_src, preferred_element_type=jnp.float32) + jnp.dot(target_rows, w_tgt, preferred_element_type=jnp.float32)
    edge_out = (edge_mid.astype(jnp.float32) + silu(update)).astype(jnp.bfloat16)
    return (edge_out, atom_out)
```

```python
import functools

import jax
import jax.numpy as jnp
from jax import lax
from jax.experimental import pallas as pl
from jax.experimental.pallas import tpu as pltpu
from jax.sharding import PartitionSpec as P

F32 = jnp.float32
BF16 = jnp.bfloat16
NT = (((1,), (1,)), ((), ()))


def silu(value):
    return value / (1.0 + jnp.exp(-value))


def dot(a, b):
    return jnp.dot(a, b, preferred_element_type=F32)


def dot_nt(a, b):
    return lax.dot_general(a, b, NT, preferred_element_type=F32)


def iota(shape, dim):
    return lax.broadcasted_iota(jnp.int32, shape, dim)


def column(row):
    return jnp.broadcast_to(row, (8, row.shape[1])).T[:, :1]


def call(kernel, out_shape, vmem, scratch=(), cost=None, name=None):
    return pl.pallas_call(
        kernel,
        out_shape=out_shape,
        scratch_shapes=list(scratch),
        compiler_params=pltpu.CompilerParams(vmem_limit_bytes=vmem),
        cost_estimate=cost,
        name=name,
    )


def cost(flops, moved):
    return pl.CostEstimate(flops=int(flops), bytes_accessed=int(moved), transcendentals=0)


def outgoing_kernel(edge_msg, w_down_t, send_rows, target, out):
    edges = edge_msg.shape[0]
    width = w_down_t.shape[0]
    peers, rows, lanes = out.shape
    half = rows - 8
    slots = peers * half * 2
    down_w = w_down_t[...]
    twice = jnp.concatenate([down_w, down_w], axis=0)
    down = silu(dot_nt(edge_msg[...], twice)).astype(BF16)
    chosen = column(send_rows[...]) == iota((slots, edges), 1)
    picked = dot(jnp.where(chosen, 1.0, 0.0).astype(BF16), down)
    picked = picked.reshape(peers, 2 * half, lanes)
    low = iota((peers, half, lanes), 2) < width
    packed = jnp.where(low, picked[:, :half], picked[:, half:])
    out[:, :half, :] = packed.astype(BF16)
    atoms = target[...]
    count = edges // lanes
    codes = [lax.shift_right_logical(atoms, 8), lax.bitwise_and(atoms, 255)]
    parts = [c[:, i * lanes : (i + 1) * lanes] for c in codes for i in range(count)]
    parts += [jnp.zeros_like(parts[0])] * (8 - len(parts))
    code_rows = jnp.concatenate(parts, axis=0).astype(F32)
    out[:, half:, :] = jnp.broadcast_to(code_rows[None], (peers, 8, lanes)).astype(BF16)


def mixer_kernel(basis, slots_flat, out, spread):
    basis_count, edges, slots = out.shape
    groups, span = slots_flat.shape
    per = edges // groups
    triplets = span // per
    total = basis.shape[1]
    rows, cols = iota((total, total), 0), iota((total, total), 1)
    order = (rows // basis_count == cols % triplets) & (rows % basis_count == cols // triplets)
    by_basis = dot(basis[...], jnp.where(order, 1.0, 0.0).astype(BF16)).astype(BF16)
    pack = 128 // triplets
    rows, cols = iota((128, span), 0), iota((128, span), 1)
    own = iota((edges, span), 0) % per == iota((edges, span), 1) // triplets
    for j in range(pack):
        tile = (rows // triplets == j) & (rows % triplets == cols % triplets)
        tile = jnp.where(tile, 1.0, 0.0).astype(BF16)
        for q in range(basis_count // pack):
            wide = dot(by_basis[:, q * 128 : (q + 1) * 128], tile)
            spread[q * pack + j] = jnp.where(own, wide, 0.0)

    def step(pair, _):
        parts = []
        for h in range(2):
            group = pair * 2 + h
            left = spread[:, pl.ds(pl.multiple_of(group * per, per), per), :]
            left = left.reshape(basis_count * per, span).astype(BF16)
            hot = iota((slots, span), 0) == slots_flat[pl.ds(group, 1), :]
            part = dot_nt(left, jnp.where(hot, 1.0, 0.0).astype(BF16))
            parts.append(part.reshape(basis_count, per, slots))
        both = jnp.concatenate(parts, axis=1).astype(BF16)
        out[:, pl.ds(pl.multiple_of(pair * 2 * per, 2 * per), 2 * per), :] = both
        return 0

    lax.fori_loop(0, groups // 2, step, 0)


def edge_kernel(received, mixer, edge_msg, w_bil_t, w_up, w_atom_in, edge_mid, message):
    peers, rows, lanes = received.shape
    half = rows - 8
    width = w_bil_t.shape[0]
    basis_count = mixer.shape[0]
    got = received[:, :half, :].astype(F32)
    swapped = pltpu.roll(got.reshape(peers * half, lanes), width, 1).reshape(got.shape)
    low = iota(got.shape, 2) < width
    first = jnp.where(low, got, swapped)
    second = jnp.where(low, swapped, got)
    table = jnp.concatenate([first, second], axis=1).reshape(peers * 2 * half, lanes)
    low = iota(table.shape, 1) < width
    even = jnp.where(low, table, 0.0).astype(BF16)
    odd = jnp.where(low, 0.0, table).astype(BF16)
    mixed = [
        (dot(mixer[2 * k], even) + dot(mixer[2 * k + 1], odd)).astype(BF16)
        for k in range(basis_count // 2)
    ]
    mixed = jnp.concatenate(mixed, axis=1)
    trip = silu(dot_nt(mixed, w_bil_t[...])).astype(BF16)
    mid = (edge_msg[...].astype(F32) + dot(trip, w_up[...])).astype(BF16)
    edge_mid[...] = mid
    sent = dot(mid, w_atom_in[...]).T.astype(BF16)
    message[...] = sent.reshape(message.shape)


def target_kernel(received, hot):
    peers, rows, lanes = received.shape
    half = rows - 8
    atoms, total = hot.shape
    edges = total // peers
    count = edges // lanes
    ids = iota((atoms, lanes), 0)

    def step(peer, _):
        codes = received[pl.ds(peer, 1), half:, :].reshape(8, lanes).astype(F32)
        for i in range(count):
            atom = codes[i : i + 1] * 256.0 + codes[count + i : count + i + 1]
            where = pl.ds(pl.multiple_of(peer * edges + i * lanes, lanes), lanes)
            hot[:, where] = jnp.where(ids == atom.astype(jnp.int32), 1.0, 0.0).astype(BF16)
        return 0

    lax.fori_loop(0, peers, step, 0)


def sum_kernel(messages, hot, out):
    peers, feats, edges = messages.shape
    total = jnp.zeros(out.shape, F32)
    for p in range(peers):
        total += dot_nt(messages[p], hot[:, p * edges : (p + 1) * edges])
    out[...] = total.astype(BF16)


def atom_kernel(owners_of, feats, wanted_count, *refs):
    piece_count = len(owners_of)
    pieces = refs[:piece_count]
    gain, atom_h, w_atom, first = refs[piece_count : piece_count + 4]
    wanted = refs[piece_count + 4 : piece_count + 4 + wanted_count]
    atom_out = refs[piece_count + 4 + wanted_count]
    sent = refs[piece_count + 5 + wanted_count : -1]
    sums = refs[-1]
    me = first[1]
    for piece, owners in zip(pieces, owners_of):
        for i, owner in enumerate(owners):
            at = pl.multiple_of(owner(me) * feats, feats)
            sums[pl.ds(at, feats), :] = piece[i * feats : (i + 1) * feats, :].astype(F32)
    values = sums[...]
    scale = lax.rsqrt(jnp.mean(values * values, axis=0, keepdims=True) + 1e-06)
    normed = (values * scale).T * gain[...]
    grown = silu(dot(normed.astype(BF16), w_atom[...]))
    rows = (atom_h[...].astype(F32) + grown).astype(BF16)
    atom_out[...] = rows
    for want, send in zip(wanted, sent):
        local = column(want[...] - first[0])
        hot = local == iota((want.shape[1], rows.shape[0]), 1)
        send[...] = dot(jnp.where(hot, 1.0, 0.0).astype(BF16), rows).astype(BF16)


def local_kernel(atom_out, source, target, first, w_src, w_tgt, out):
    rows = atom_out[...]
    edges = source.shape[1]
    ids = iota((edges, rows.shape[0]), 1)

    def pick(index):
        hot = column(index[...] - first[0]) == ids
        return dot(jnp.where(hot, 1.0, 0.0).astype(BF16), rows).astype(BF16)

    out[...] = dot(pick(source), w_src[...]) + dot(pick(target), w_tgt[...])


def final_kernel(*refs):
    out = refs[-1]
    partial, edge_mid, w_src = refs[:3]
    rows = refs[3:-1]
    update = partial[...]
    if rows:
        got = rows[0][...].astype(F32)
        for r in rows[1:]:
            got = got + r[...].astype(F32)
        update = update + dot(got.astype(BF16), w_src[...])
    out[...] = (edge_mid[...].astype(F32) + silu(update)).astype(BF16)


def stage_factors(wide):
    stages = []
    left = wide
    size = min(4, max(1, wide // 4))
    stride = wide
    for f in (size, max(1, wide // (2 * size)), 2):
        if f > 1 and left % f == 0:
            stride //= f
            left //= f
            stages.append((stride, f))
    return stages


def per_device(
    wide,
    narrow,
    edge_msg,
    basis,
    atom_h,
    edge_source,
    edge_target,
    send_rows,
    trip_slot,
    w_down,
    w_bil,
    w_up,
    w_atom_in,
    atom_gain,
    w_atom,
    w_src,
    w_tgt,
):
    edges, de = edge_msg.shape
    width = w_down.shape[1]
    basis_count = w_bil.shape[0] // width
    triplets = trip_slot.shape[1]
    atoms, da = atom_h.shape
    slots = send_rows.shape[1]
    cap = slots // wide
    feats = da // wide
    lanes = 2 * width
    big = (24 << 20) if slots <= 512 else (60 << 20)
    shape = jax.ShapeDtypeStruct

    first_atom = lax.axis_index("narrow") * atoms
    place = jnp.stack([first_atom, lax.axis_index("wide")]).astype(jnp.int32)
    source = edge_source.reshape(1, edges)
    target = edge_target.reshape(1, edges)

    outgoing = call(
        outgoing_kernel, shape((wide, cap // 2 + 8, lanes), BF16), big, name="outgoing"
    )(edge_msg, w_down.T, send_rows, target - first_atom)
    received = lax.all_to_all(outgoing, "wide", split_axis=0, concat_axis=0, tiled=True)

    wanted = [
        lax.ppermute(source, "narrow", [(i, (i + k) % narrow) for i in range(narrow)])
        for k in range(1, narrow)
    ]
    per = 256 // triplets
    slots_flat = trip_slot.reshape(edges // per, per * triplets)
    mixer = call(
        mixer_kernel,
        shape((basis_count, edges, slots), BF16),
        big,
        scratch=[pltpu.VMEM((basis_count, edges, per * triplets), F32)],
        cost=cost(2 * basis_count * edges * slots * 256, 6 << 20),
        name="mixer",
    )(basis, slots_flat)

    edge_mid, message = call(
        edge_kernel,
        (shape((edges, de), BF16), shape((wide, feats, edges), BF16)),
        big,
        name="edge",
    )(received, mixer, edge_msg, w_bil.T, w_up, w_atom_in)
    messages = lax.all_to_all(message, "wide", split_axis=0, concat_axis=0, tiled=True)
    hot = call(
        target_kernel,
        shape((atoms, wide * edges), BF16),
        big,
        cost=cost(1 << 24, 5 << 20),
        name="targets",
    )(received)
    share = call(sum_kernel, shape((feats, atoms), BF16), big, name="sums")(messages, hot)

    groups = [(share, [lambda me: me])]
    stages = stage_factors(wide)
    for number, (stride, size) in enumerate(stages):
        def moved(k, stride=stride, size=size):
            def owner(me):
                place_in = (me // stride) % size
                return me + ((place_in + size - k) % size - place_in) * stride
            return owner

        fresh = []
        for value, owners in groups:
            got = [(value, owners)]
            for k in range(1, size):
                pairs = []
                for i in range(wide):
                    at = (i // stride) % size
                    pairs.append((i, i + ((at + k) % size - at) * stride))
                back = moved(k)
                got.append(
                    (
                        lax.ppermute(value, "wide", pairs),
                        [lambda me, o=o, back=back: o(back(me)) for o in owners],
                    )
                )
            if size > 2:
                fresh.append(
                    (
                        jnp.concatenate([v for v, _ in got], axis=0),
                        [o for _, os in got for o in os],
                    )
                )
            else:
                fresh.extend(got)
        groups = fresh

    smem = pl.BlockSpec(memory_space=pltpu.SMEM)
    vmem = pl.BlockSpec(memory_space=pltpu.VMEM)
    pieces = [v for v, _ in groups]
    owners_of = [o for _, o in groups]
    outs = pl.pallas_call(
        functools.partial(atom_kernel, owners_of, feats, len(wanted)),
        out_shape=[shape((atoms, da), BF16)] + [shape((edges, da), BF16)] * len(wanted),
        in_specs=[vmem] * (len(pieces) + 3) + [smem] + [vmem] * len(wanted),
        out_specs=[vmem] * (1 + len(wanted)),
        scratch_shapes=[pltpu.VMEM((da, atoms), F32)],
        compiler_params=pltpu.CompilerParams(vmem_limit_bytes=big),
        name="atoms",
    )(*pieces, atom_gain.reshape(1, da), atom_h, w_atom, place, *wanted)
    atom_out, asked = outs[0], outs[1:]
    rows = [
        lax.ppermute(a, "narrow", [(i, (i - k) % narrow) for i in range(narrow)])
        for k, a in enumerate(asked, start=1)
    ]
    partial = pl.pallas_call(
        local_kernel,
        out_shape=shape((edges, de), F32),
        in_specs=[vmem, vmem, vmem, smem, vmem, vmem],
        out_specs=vmem,
        compiler_params=pltpu.CompilerParams(vmem_limit_bytes=big),
        cost_estimate=cost(4 * edges * da * de + 4 * edges * da * atoms, 4 << 20),
        name="local",
    )(atom_out, source, target, place, w_src, w_tgt)
    edge_out = call(final_kernel, shape((edges, de), BF16), big, name="final")(
        partial, edge_mid, w_src, *rows
    )
    return (edge_out, atom_out)


def solution(mesh):
    placed = (
        P(("wide", "narrow"), None),
        P(("wide", "narrow"), None),
        P("narrow", None),
        P(("wide", "narrow")),
        P(("wide", "narrow")),
        P(("wide", "narrow"), None),
        P(("wide", "narrow"), None),
        P(),
        P(),
        P(),
        P(),
        P(),
        P(),
        P(),
        P(),
    )
    return jax.shard_map(
        functools.partial(per_device, mesh.shape["wide"], mesh.shape["narrow"]),
        mesh=mesh,
        in_specs=placed,
        out_specs=(P(("wide", "narrow"), None), P("narrow", None)),
        check_vma=False,
    )
```

```python
import functools

import jax
import jax.numpy as jnp
from jax import lax
from jax.experimental import pallas as pl
from jax.experimental.pallas import tpu as pltpu
from jax.sharding import PartitionSpec as P

F32 = jnp.float32
BF16 = jnp.bfloat16
NT = (((1,), (1,)), ((), ()))


def silu(value):
    return value / (1.0 + jnp.exp(-value))


def dot(a, b):
    return jnp.dot(a, b, preferred_element_type=F32)


def dot_nt(a, b):
    return lax.dot_general(a, b, NT, preferred_element_type=F32)


def iota(shape, dim):
    return lax.broadcasted_iota(jnp.int32, shape, dim)


def column(row):
    return jnp.broadcast_to(row, (8, row.shape[1])).T[:, :1]


VMEM = pl.BlockSpec(memory_space=pltpu.VMEM)
HBM = pl.BlockSpec(memory_space=pltpu.HBM)


def call(kernel, ins, outs, out_shape, vmem, scratch=(), cost=None, name=None):
    def kept(spec, leaf):
        return pltpu.HBM(leaf.shape, leaf.dtype) if spec is HBM else leaf

    many = isinstance(out_shape, (list, tuple))
    out_shape = [kept(o, s) for o, s in zip(outs, out_shape)] if many else kept(outs, out_shape)
    run = pl.pallas_call(
        kernel,
        out_shape=out_shape,
        in_specs=list(ins),
        out_specs=outs,
        scratch_shapes=list(scratch),
        compiler_params=pltpu.CompilerParams(vmem_limit_bytes=vmem),
        cost_estimate=cost,
        name=name,
    )

    def apply(*args):
        held = [
            pltpu.with_memory_space_constraint(a, pltpu.HBM) if spec is HBM else a
            for spec, a in zip(ins, args)
        ]
        return run(*held)

    return apply


def cost(flops, moved):
    return pl.CostEstimate(flops=int(flops), bytes_accessed=int(moved), transcendentals=0)


def place(axis, size):
    return lax.axis_index(axis) * size


def one_hot(index, count):
    hot = column(index) == iota((index.shape[1], count), 1)
    return jnp.where(hot, 1.0, 0.0).astype(BF16)


def outgoing_kernel(atoms, edge_hbm, w_hbm, rows_hbm, target_hbm, out, edge, w, rows, target, sems):
    edges = edge.shape[0]
    width = w.shape[0]
    peers, block, lanes = out.shape
    half = block - 8
    slots = peers * half * 2
    chunks = sems.shape[0] - 3
    step = edges // chunks
    copies = [
        pltpu.make_async_copy(rows_hbm, rows, sems.at[0]),
        pltpu.make_async_copy(target_hbm, target, sems.at[1]),
        pltpu.make_async_copy(w_hbm, w, sems.at[2]),
    ]
    for i in range(chunks):
        part = pl.ds(i * step, step)
        copies.append(pltpu.make_async_copy(edge_hbm.at[part, :], edge.at[part, :], sems.at[3 + i]))
    for c in copies:
        c.start()
    copies[0].wait()
    copies[1].wait()
    hot = one_hot(rows[...], edges)
    local = target[...] - place("narrow", atoms)
    count = edges // lanes
    codes = [lax.shift_right_logical(local, 8), lax.bitwise_and(local, 255)]
    parts = [c[:, i * lanes : (i + 1) * lanes] for c in codes for i in range(count)]
    parts += [jnp.zeros_like(parts[0])] * (8 - len(parts))
    code_rows = jnp.concatenate(parts, axis=0).astype(F32)
    out[:, half:, :] = jnp.broadcast_to(code_rows[None], (peers, 8, lanes)).astype(BF16)
    copies[2].wait()
    down_w = w[...]
    twice = jnp.concatenate([down_w, down_w], axis=0)
    down = []
    for i in range(chunks):
        copies[3 + i].wait()
        down.append(silu(dot_nt(edge[i * step : (i + 1) * step, :], twice)).astype(BF16))
    picked = dot(hot, jnp.concatenate(down, axis=0))
    picked = picked.reshape(peers, 2 * half, lanes)
    low = iota((peers, half, lanes), 2) < width
    packed = jnp.where(low, picked[:, :half], picked[:, half:])
    out[:, :half, :] = packed.astype(BF16)


def start_first(copies):
    def go(_, carry):
        for c in copies:
            c.start()
        return carry

    lax.fori_loop(0, jnp.minimum(lax.axis_index("wide"), 0) + 1, go, 0)


def mixer_kernel(
    cap, basis_hbm, slots_hbm, kept, rest_hbm, basis, slots_t, flat, spread, rest, sems
):
    kept_count, edges, slots = kept.shape
    basis_count = kept_count + rest_hbm.shape[0]
    triplets = slots_t.shape[0]
    groups, span = flat.shape
    per = edges // groups
    total = basis.shape[1]
    fetch = [
        pltpu.make_async_copy(slots_hbm, slots_t, sems.at[0]),
        pltpu.make_async_copy(basis_hbm, basis, sems.at[1]),
    ]
    start_first(fetch)
    rows, cols = iota((total, total), 0), iota((total, total), 1)
    order = (rows // basis_count == cols % triplets) & (rows % basis_count == cols // triplets)
    order = jnp.where(order, 1.0, 0.0).astype(BF16)
    own = iota((edges, span), 0) % per == iota((edges, span), 1) // triplets
    fetch[0].wait()
    half = cap // 2
    slot = slots_t[...]
    slot = (slot // half) % 2 * (slots // 2) + slot // cap * half + slot % half
    slot = slot.T
    tile = jnp.where(iota((triplets, span), 0) == iota((triplets, span), 1) % triplets, 1.0, 0.0)
    tile = tile.astype(BF16)
    high = lax.shift_right_logical(slot, 8).astype(F32).astype(BF16)
    low = lax.bitwise_and(slot, 255).astype(F32).astype(BF16)
    wide = jnp.where(own, dot(high, tile) * 256.0 + dot(low, tile), 0.0)
    flat[...] = jnp.sum(wide.reshape(groups, per, span), axis=1).astype(jnp.int32)
    fetch[1].wait()
    by_basis = dot(basis[...], order).astype(BF16)
    pack = 128 // triplets
    rows, cols = iota((128, span), 0), iota((128, span), 1)
    for j in range(pack):
        tile = (rows // triplets == j) & (rows % triplets == cols % triplets)
        tile = jnp.where(tile, 1.0, 0.0).astype(BF16)
        for q in range(basis_count // pack):
            wide = dot(by_basis[:, q * 128 : (q + 1) * 128], tile)
            spread[q * pack + j] = jnp.where(own, wide, 0.0)

    def one(pair):
        parts = []
        for h in range(2):
            group = pair * 2 + h
            left = spread[:, pl.ds(pl.multiple_of(group * per, per), per), :]
            left = left.reshape(basis_count * per, span).astype(BF16)
            hot = iota((slots, span), 0) == flat[pl.ds(group, 1), :]
            part = dot_nt(left, jnp.where(hot, 1.0, 0.0).astype(BF16))
            parts.append(part.reshape(basis_count, per, slots))
        both = jnp.concatenate(parts, axis=1).astype(BF16)
        at = pl.ds(pl.multiple_of(pair * 2 * per, 2 * per), 2 * per)
        kept[:, at, :] = both[:kept_count]
        rest[:, at, :] = both[kept_count:]

    def step(i, _):
        one(2 * i)
        one(2 * i + 1)
        return 0

    chunks = sems.shape[0] - 2
    steps = groups // 4 // chunks
    copies = []
    for c in range(chunks):
        lax.fori_loop(c * steps, (c + 1) * steps, step, 0)
        part = pl.ds(c * steps * 4 * per, steps * 4 * per)
        copies.append(
            pltpu.make_async_copy(rest.at[:, part, :], rest_hbm.at[:, part, :], sems.at[2 + c])
        )
        copies[-1].start()
    for c in copies:
        c.wait()


def edge_kernel(
    received,
    kept,
    rest_hbm,
    edge_hbm,
    w_bil_hbm,
    w_up_hbm,
    w_atom_hbm,
    mid_hbm,
    message,
    rest,
    edge_msg,
    w_bil_t,
    w_up,
    w_atom_in,
    edge_mid,
    sems,
):
    peers, rows, lanes = received.shape
    half = rows - 8
    width = w_bil_t.shape[0]
    pairs = [
        (rest_hbm, rest),
        (w_bil_hbm, w_bil_t),
        (w_up_hbm, w_up),
        (edge_hbm, edge_msg),
        (w_atom_hbm, w_atom_in),
    ]
    copies = [pltpu.make_async_copy(a, b, sems.at[i]) for i, (a, b) in enumerate(pairs)]
    start_first(copies)
    got = received[:, :half, :].astype(F32).reshape(peers * half, lanes).T
    table = jnp.concatenate([got[:width], got[width:]], axis=1).astype(BF16)
    mixed = [dot_nt(table, kept[k]).astype(BF16) for k in range(kept.shape[0])]
    copies[0].wait()
    mixed += [dot_nt(table, rest[k]).astype(BF16) for k in range(rest.shape[0])]
    mixed = jnp.concatenate(mixed, axis=0)
    copies[1].wait()
    trip = silu(dot(w_bil_t[...], mixed)).T.astype(BF16)
    copies[2].wait()
    copies[3].wait()
    mid = (edge_msg[...].astype(F32) + dot(trip, w_up[...])).astype(BF16)
    edge_mid[...] = mid
    store = pltpu.make_async_copy(edge_mid, mid_hbm, sems.at[len(pairs)])
    store.start()
    copies[4].wait()
    sent = dot(mid, w_atom_in[...]).T.astype(BF16)
    message[...] = sent.reshape(message.shape)
    store.wait()


def picks_kernel(count, *refs):
    wanted = refs[:count]
    atom_h = refs[count]
    hots, olds = refs[count + 1 : 2 * count + 1], refs[2 * count + 1 :]
    atoms = atom_h.shape[0]
    for want, hot, old in zip(wanted, hots, olds):
        chosen = one_hot(want[...] - place("narrow", atoms), atoms)
        hot[...] = chosen
        old[...] = dot(chosen, atom_h[...]).astype(BF16)


def sum_kernel(messages, received, *refs):
    out = refs[-1]
    peers, feats, edges = messages.shape
    _, rows, lanes = received.shape
    half = rows - 8
    count = edges // lanes
    total = jnp.zeros(out.shape, F32)
    ids = iota((out.shape[1], lanes), 0).astype(F32)
    for p in range(peers):
        codes = received[p, half:, :].astype(F32)
        hot = [
            jnp.where(ids == codes[i : i + 1] * 256.0 + codes[count + i : count + i + 1], 1.0, 0.0)
            for i in range(count)
        ]
        total += dot_nt(messages[p], jnp.concatenate(hot, axis=1).astype(BF16))
    out[...] = total.astype(BF16)


def asked_kernel(owners_of, feats, count, *refs):
    pieces = refs[: len(owners_of)]
    gain, w_atom = refs[len(owners_of) : len(owners_of) + 2]
    at = len(owners_of) + 2
    hots, olds = refs[at : at + count], refs[at + count : at + 2 * count]
    normed_out = refs[at + 2 * count]
    sent = refs[at + 2 * count + 1 : -1]
    sums = refs[-1]
    me = lax.axis_index("wide")
    for piece, owners in zip(pieces, owners_of):
        for i, owner in enumerate(owners):
            to = pl.multiple_of(owner(me) * feats, feats)
            sums[pl.ds(to, feats), :] = piece[i * feats : (i + 1) * feats, :].astype(F32)
    values = sums[...]
    scale = lax.rsqrt(jnp.mean(values * values, axis=0, keepdims=True) + 1e-06)
    normed = (values * scale * column_f32(gain[...])).astype(BF16)
    normed_out[...] = normed
    for hot, old, send in zip(hots, olds, sent):
        rows = dot_nt(hot[...], normed).astype(BF16)
        grown = silu(dot(rows, w_atom[...]))
        send[...] = (old[...].astype(F32) + grown).astype(BF16)


def column_f32(row):
    return jnp.broadcast_to(row, (8, row.shape[1])).T[:, :1]


def local_kernel(
    normed_t, atom_h, w_atom, source, target, w_src, w_tgt, atom_hbm, out, atom_out, sem
):
    atoms = atom_h.shape[0]
    first = place("narrow", atoms)
    same = iota((atoms, atoms), 0) == iota((atoms, atoms), 1)
    normed = dot_nt(jnp.where(same, 1.0, 0.0).astype(BF16), normed_t[...]).astype(BF16)
    grown = silu(dot(normed, w_atom[...]))
    rows = (atom_h[...].astype(F32) + grown).astype(BF16)
    atom_out[...] = rows
    store = pltpu.make_async_copy(atom_out, atom_hbm, sem)
    store.start()
    sources = dot(one_hot(source[...] - first, atoms), rows).astype(BF16)
    targets = dot(one_hot(target[...] - first, atoms), rows).astype(BF16)
    out[...] = dot(sources, w_src[...]) + dot(targets, w_tgt[...])
    store.wait()


def final_kernel(count, *refs):
    partial, mid, w_src = refs[:3]
    rows = refs[3 : 3 + count]
    out = refs[3 + count]
    update = partial[...]
    if rows:
        got = rows[0][...].astype(F32)
        for r in rows[1:]:
            got = got + r[...].astype(F32)
        update = update + dot(got.astype(BF16), w_src[...])
    out[...] = (mid[...].astype(F32) + silu(update)).astype(BF16)


def stage_factors(wide):
    stages = []
    left = wide
    size = min(4, max(1, wide // 4))
    stride = wide
    for f in (size, max(1, wide // (2 * size)), 2):
        if f > 1 and left % f == 0:
            stride //= f
            left //= f
            stages.append((stride, f))
    return stages


def per_device(
    wide,
    narrow,
    edge_msg,
    basis,
    atom_h,
    edge_source,
    edge_target,
    send_rows,
    trip_slot,
    w_down,
    w_bil,
    w_up,
    w_atom_in,
    atom_gain,
    w_atom,
    w_src,
    w_tgt,
):
    edges, de = edge_msg.shape
    width = w_down.shape[1]
    basis_count = w_bil.shape[0] // width
    triplets = trip_slot.shape[1]
    atoms, da = atom_h.shape
    slots = send_rows.shape[1]
    cap = slots // wide
    feats = da // wide
    lanes = 2 * width
    big = (24 << 20) if slots <= 512 else (60 << 20)
    shape = jax.ShapeDtypeStruct

    source = edge_source.reshape(1, edges)
    target = edge_target.reshape(1, edges)
    dma = pltpu.SemaphoreType.DMA

    outgoing = call(
        functools.partial(outgoing_kernel, atoms),
        [HBM] * 4,
        VMEM,
        shape((wide, cap // 2 + 8, lanes), BF16),
        big,
        scratch=[
            pltpu.VMEM((edges, de), BF16),
            pltpu.VMEM((width, de), BF16),
            pltpu.VMEM((1, slots), jnp.int32),
            pltpu.VMEM((1, edges), jnp.int32),
            dma((7,)),
        ],
        name="outgoing",
    )(edge_msg, w_down.T, send_rows, target)
    received = lax.all_to_all(outgoing, "wide", split_axis=0, concat_axis=0, tiled=True)

    per = 256 // triplets
    kept = max(1, min(basis_count - 1, (3 << 20) // (edges * slots * 2)))
    rest_shape = (basis_count - kept, edges, slots)
    mixer = call(
        functools.partial(mixer_kernel, cap),
        [HBM, HBM],
        [VMEM, HBM],
        [shape((kept, edges, slots), BF16), shape(rest_shape, BF16)],
        big,
        scratch=[
            pltpu.VMEM(basis.shape, BF16),
            pltpu.VMEM((triplets, edges), jnp.int32),
            pltpu.VMEM((edges // per, per * triplets), jnp.int32),
            pltpu.VMEM((basis_count, edges, per * triplets), F32),
            pltpu.VMEM(rest_shape, BF16),
            dma((6,)),
        ],
        cost=cost(2 * basis_count * edges * slots * 256, 6 << 20),
        name="mixer",
    )(basis, trip_slot.T)

    edge_mid, message = call(
        edge_kernel,
        [VMEM] * 2 + [HBM] * 5,
        [HBM, VMEM],
        (shape((edges, de), BF16), shape((wide, feats, edges), BF16)),
        big,
        scratch=[
            pltpu.VMEM(rest_shape, BF16),
            pltpu.VMEM((edges, de), BF16),
            pltpu.VMEM((width, basis_count * width), BF16),
            pltpu.VMEM(w_up.shape, BF16),
            pltpu.VMEM(w_atom_in.shape, BF16),
            pltpu.VMEM((edges, de), BF16),
            dma((6,)),
        ],
        name="edge",
    )(received, *mixer, edge_msg, w_bil.T, w_up, w_atom_in)
    messages = lax.all_to_all(message, "wide", split_axis=0, concat_axis=0, tiled=True)

    source_late, _ = lax.optimization_barrier((source, message))
    wanted = [
        lax.ppermute(source_late, "narrow", [(i, (i + k) % narrow) for i in range(narrow)])
        for k in range(1, narrow)
    ]
    picks = []
    if wanted:
        picks = call(
            functools.partial(picks_kernel, len(wanted)),
            [VMEM] * (len(wanted) + 1),
            [VMEM] * (2 * len(wanted)),
            [shape((edges, atoms), BF16)] * len(wanted) + [shape((edges, da), BF16)] * len(wanted),
            big,
            name="picks",
        )(*wanted, atom_h)
    share = call(
        sum_kernel,
        [VMEM, VMEM] + [pl.BlockSpec(memory_space=pl.ANY)] * len(picks),
        VMEM,
        shape((feats, atoms), BF16),
        big,
        name="sums",
    )(messages, received, *picks)

    groups = [(share, [lambda me: me])]
    stages = stage_factors(wide)
    for number, (stride, size) in enumerate(stages):
        mirror = size & (size - 1) == 0

        def turned(at, k, size=size, mirror=mirror):
            return at ^ k if mirror else (at + k) % size

        def moved(k, stride=stride, size=size, turned=turned, mirror=mirror):
            def owner(me):
                at = (me // stride) % size
                return me + (turned(at, k if mirror else size - k) - at) * stride
            return owner

        fresh = []
        for value, owners in groups:
            got = [(value, owners)]
            for k in range(1, size):
                pairs = []
                for i in range(wide):
                    at = (i // stride) % size
                    pairs.append((i, i + (turned(at, k) - at) * stride))
                back = moved(k)
                got.append(
                    (
                        lax.ppermute(value, "wide", pairs),
                        [lambda me, o=o, back=back: o(back(me)) for o in owners],
                    )
                )
            if size > 2:
                fresh.append(
                    (
                        jnp.concatenate([v for v, _ in got], axis=0),
                        [o for _, os in got for o in os],
                    )
                )
            else:
                fresh.extend(got)
        groups = fresh

    pieces = [v for v, _ in groups]
    owners_of = [o for _, o in groups]
    outs = call(
        functools.partial(asked_kernel, owners_of, feats, len(wanted)),
        [VMEM] * (len(pieces) + 2 + len(picks)),
        [VMEM] * (1 + len(wanted)),
        [shape((da, atoms), BF16)] + [shape((edges, da), BF16)] * len(wanted),
        big,
        scratch=[pltpu.VMEM((da, atoms), F32)],
        name="asked",
    )(*pieces, atom_gain.reshape(1, da), w_atom, *picks)
    normed, asked = outs[0], outs[1:]
    rows = [
        lax.ppermute(a, "narrow", [(i, (i - k) % narrow) for i in range(narrow)])
        for k, a in enumerate(asked, start=1)
    ]
    atom_out, partial = call(
        local_kernel,
        [VMEM] * 7,
        [HBM, VMEM],
        (shape((atoms, da), BF16), shape((edges, de), F32)),
        big,
        scratch=[pltpu.VMEM((atoms, da), BF16), dma],
        cost=cost(4 * edges * da * de + 8 * edges * da * atoms, 4 << 20),
        name="local",
    )(normed, atom_h, w_atom, source, target, w_src, w_tgt)
    edge_out = call(
        functools.partial(final_kernel, len(rows)),
        [VMEM] * (3 + len(rows)),
        VMEM,
        shape((edges, de), BF16),
        big,
        name="final",
    )(partial, edge_mid, w_src, *rows)
    return (edge_out, atom_out)


def solution(mesh):
    placed = (
        P(("wide", "narrow"), None),
        P(("wide", "narrow"), None),
        P("narrow", None),
        P(("wide", "narrow")),
        P(("wide", "narrow")),
        P(("wide", "narrow"), None),
        P(("wide", "narrow"), None),
        P(),
        P(),
        P(),
        P(),
        P(),
        P(),
        P(),
        P(),
    )
    return jax.shard_map(
        functools.partial(per_device, mesh.shape["wide"], mesh.shape["narrow"]),
        mesh=mesh,
        in_specs=placed,
        out_specs=(P(("wide", "narrow"), None), P("narrow", None)),
        check_vma=False,
    )
```

```python
import functools

import jax
import jax.numpy as jnp
from jax import lax
from jax.experimental import pallas as pl
from jax.experimental.pallas import tpu as pltpu
from jax.sharding import PartitionSpec as P

F32 = jnp.float32
BF16 = jnp.bfloat16
NT = (((1,), (1,)), ((), ()))


def silu(value):
    return value / (1.0 + jnp.exp(-value))


def dot(a, b):
    return jnp.dot(a, b, preferred_element_type=F32)


def dot_nt(a, b):
    return lax.dot_general(a, b, NT, preferred_element_type=F32)


def iota(shape, dim):
    return lax.broadcasted_iota(jnp.int32, shape, dim)


def column(row):
    return jnp.broadcast_to(row, (8, row.shape[1])).T[:, :1]


VMEM = pl.BlockSpec(memory_space=pltpu.VMEM)
HBM = pl.BlockSpec(memory_space=pltpu.HBM)


def quotient(value, by):
    if by & (by - 1) == 0:
        return lax.shift_right_logical(value, by.bit_length() - 1)
    return lax.div(value, jnp.int32(by))


def remainder(value, by):
    if by & (by - 1) == 0:
        return lax.bitwise_and(value, by - 1)
    return lax.rem(value, jnp.int32(by))


def call(kernel, ins, outs, out_shape, vmem, scratch=(), cost=None, name=None):
    def kept(spec, leaf):
        return pltpu.HBM(leaf.shape, leaf.dtype) if spec is HBM else leaf

    many = isinstance(out_shape, (list, tuple))
    out_shape = [kept(o, s) for o, s in zip(outs, out_shape)] if many else kept(outs, out_shape)
    run = pl.pallas_call(
        kernel,
        out_shape=out_shape,
        in_specs=list(ins),
        out_specs=outs,
        scratch_shapes=list(scratch),
        compiler_params=pltpu.CompilerParams(vmem_limit_bytes=vmem),
        cost_estimate=cost,
        name=name,
    )

    def apply(*args):
        held = [
            pltpu.with_memory_space_constraint(a, pltpu.HBM) if spec is HBM else a
            for spec, a in zip(ins, args)
        ]
        return run(*held)

    return apply


def cost(flops, moved):
    return pl.CostEstimate(flops=int(flops), bytes_accessed=int(moved), transcendentals=0)


def place(axis, size):
    return lax.axis_index(axis) * size


def one_hot(index, count):
    hot = column(index) == iota((index.shape[1], count), 1)
    return jnp.where(hot, 1.0, 0.0).astype(BF16)


def outgoing_kernel(atoms, edge_hbm, w_hbm, rows_hbm, target_hbm, out, edge, w, rows, target, sems):
    edges = edge.shape[0]
    width = w.shape[0]
    peers, block, lanes = out.shape
    half = block - 8
    slots = peers * half * 2
    chunks = sems.shape[0] - 3
    step = edges // chunks
    copies = [
        pltpu.make_async_copy(rows_hbm, rows, sems.at[0]),
        pltpu.make_async_copy(target_hbm, target, sems.at[1]),
        pltpu.make_async_copy(w_hbm, w, sems.at[2]),
    ]
    for i in range(chunks):
        part = pl.ds(i * step, step)
        copies.append(pltpu.make_async_copy(edge_hbm.at[part, :], edge.at[part, :], sems.at[3 + i]))
    for c in copies:
        c.start()
    copies[0].wait()
    copies[1].wait()
    hot = one_hot(rows[...], edges)
    local = target[...] - place("narrow", atoms)
    count = edges // lanes
    codes = [lax.shift_right_logical(local, 8), lax.bitwise_and(local, 255)]
    parts = [c[:, i * lanes : (i + 1) * lanes] for c in codes for i in range(count)]
    parts += [jnp.zeros_like(parts[0])] * (8 - len(parts))
    code_rows = jnp.concatenate(parts, axis=0).astype(F32)
    out[:, half:, :] = jnp.broadcast_to(code_rows[None], (peers, 8, lanes)).astype(BF16)
    copies[2].wait()
    down_w = w[...]
    twice = jnp.concatenate([down_w, down_w], axis=0)
    down = []
    for i in range(chunks):
        copies[3 + i].wait()
        down.append(silu(dot_nt(edge[i * step : (i + 1) * step, :], twice)).astype(BF16))
    picked = dot(hot, jnp.concatenate(down, axis=0))
    picked = picked.reshape(peers, 2 * half, lanes)
    low = iota((peers, half, lanes), 2) < width
    packed = jnp.where(low, picked[:, :half], picked[:, half:])
    out[:, :half, :] = packed.astype(BF16)


def start_first(copies):
    def go(_, carry):
        for c in copies:
            c.start()
        return carry

    lax.fori_loop(0, jnp.minimum(lax.axis_index("wide"), 0) + 1, go, 0)


def mixer_kernel(
    cap, basis_hbm, slots_hbm, kept, rest_hbm, basis, slots_t, flat, spread, rest, sems
):
    kept_count, edges, slots = kept.shape
    basis_count = kept_count + rest_hbm.shape[0]
    triplets = slots_t.shape[0]
    groups, span = flat.shape
    per = edges // groups
    total = basis.shape[1]
    fetch = [
        pltpu.make_async_copy(slots_hbm, slots_t, sems.at[0]),
        pltpu.make_async_copy(basis_hbm, basis, sems.at[1]),
    ]
    start_first(fetch)
    rows, cols = iota((total, total), 0), iota((total, total), 1)
    order = quotient(rows, basis_count) + remainder(rows, basis_count) * triplets == cols
    order = jnp.where(order, 1.0, 0.0).astype(BF16)
    own = remainder(iota((edges, span), 0), per) == quotient(iota((edges, span), 1), triplets)
    fetch[0].wait()
    half = cap // 2
    slot = slots_t[...]
    slot = (
        remainder(quotient(slot, half), 2) * (slots // 2)
        + quotient(slot, cap) * half
        + remainder(slot, half)
    )
    slot = slot.T
    turn = remainder(iota((triplets, span), 1), triplets)
    tile = jnp.where(iota((triplets, span), 0) == turn, 1.0, 0.0)
    tile = tile.astype(BF16)
    high = lax.shift_right_logical(slot, 8).astype(F32).astype(BF16)
    low = lax.bitwise_and(slot, 255).astype(F32).astype(BF16)
    wide = jnp.where(own, dot(high, tile) * 256.0 + dot(low, tile), 0.0)
    flat[...] = jnp.sum(wide.reshape(groups, per, span), axis=1).astype(jnp.int32)
    fetch[1].wait()
    by_basis = dot(basis[...], order)
    pack = 128 // triplets
    turn = remainder(iota((edges, 128), 0), pack)
    for q in range(total // 128):
        lanes = by_basis[:, q * 128 : (q + 1) * 128]
        turned = lanes
        for r in range(1, pack):
            turned = jnp.where(turn == r, pltpu.roll(lanes, r * triplets, 1), turned)
        spread[:, q * 128 : (q + 1) * 128] = turned
    row, lane = iota((per, 128), 0), quotient(iota((per, 128), 1), triplets)
    mine = [row == lane + c * pack for c in range(span // 128)]

    def one(pair):
        parts = []
        for h in range(2):
            group = pair * 2 + h
            values = spread[pl.ds(pl.multiple_of(group * per, per), per), :]
            left = []
            for k in range(basis_count):
                q, j = k // pack, k % pack
                lanes = values[:, q * 128 : (q + 1) * 128]
                if j:
                    lanes = pltpu.roll(lanes, 128 - j * triplets, 1)
                left.append(jnp.concatenate([jnp.where(m, lanes, 0.0) for m in mine], axis=1))
            left = jnp.concatenate(left, axis=0).astype(BF16)
            hot = iota((slots, span), 0) == flat[pl.ds(group, 1), :]
            part = dot_nt(left, jnp.where(hot, 1.0, 0.0).astype(BF16))
            parts.append(part.reshape(basis_count, per, slots))
        both = jnp.concatenate(parts, axis=1).astype(BF16)
        at = pl.ds(pl.multiple_of(pair * 2 * per, 2 * per), 2 * per)
        kept[:, at, :] = both[:kept_count]
        rest[:, at, :] = both[kept_count:]

    unroll = 4

    def step(i, _):
        for u in range(unroll):
            one(unroll * i + u)
        return 0

    chunks = sems.shape[0] - 2
    steps = groups // 2 // unroll // chunks
    copies = []
    for c in range(chunks):
        lax.fori_loop(c * steps, (c + 1) * steps, step, 0)
        size = steps * unroll * 2 * per
        part = pl.ds(c * size, size)
        copies.append(
            pltpu.make_async_copy(rest.at[:, part, :], rest_hbm.at[:, part, :], sems.at[2 + c])
        )
        copies[-1].start()
    for c in copies:
        c.wait()


def edge_kernel(
    received,
    kept,
    rest_hbm,
    edge_hbm,
    w_bil_hbm,
    w_up_hbm,
    w_atom_hbm,
    mid_hbm,
    *refs,
):
    *quarters, rest, edge_msg, w_bil_t, w_up, w_atom_in, edge_mid, message, sems = refs
    peers, rows, lanes = received.shape
    half = rows - 8
    width = w_bil_t.shape[0]
    pairs = [
        (rest_hbm, rest),
        (w_bil_hbm, w_bil_t),
        (w_up_hbm, w_up),
        (edge_hbm, edge_msg),
        (w_atom_hbm, w_atom_in),
    ]
    copies = [pltpu.make_async_copy(a, b, sems.at[i]) for i, (a, b) in enumerate(pairs)]
    start_first(copies)
    got = received[:, :half, :].astype(F32).reshape(peers * half, lanes).T
    table = jnp.concatenate([got[:width], got[width:]], axis=1).astype(BF16)
    mixed = [dot_nt(table, kept[k]).astype(BF16) for k in range(kept.shape[0])]
    copies[0].wait()
    mixed += [dot_nt(table, rest[k]).astype(BF16) for k in range(rest.shape[0])]
    mixed = jnp.concatenate(mixed, axis=0)
    copies[1].wait()
    trip = silu(dot(w_bil_t[...], mixed)).T.astype(BF16)
    copies[2].wait()
    copies[3].wait()
    mid = (edge_msg[...].astype(F32) + dot(trip, w_up[...])).astype(BF16)
    edge_mid[...] = mid
    store = pltpu.make_async_copy(edge_mid, mid_hbm, sems.at[len(pairs)])
    store.start()
    copies[4].wait()
    message[...] = dot(mid, w_atom_in[...]).T
    part = message.shape[0] // len(quarters)
    mine = lax.axis_index("wide") % len(quarters)
    for q, quarter in enumerate(quarters):
        at = pl.multiple_of((mine ^ q) * part, part)
        quarter[...] = message[pl.ds(at, part), :].astype(BF16)
    store.wait()


def picks_kernel(order, feats, count, *refs):
    wanted = refs[:count]
    atom_h, gain, w_hbm = refs[count : count + 3]
    hots = refs[count + 3 : 2 * count + 3]
    olds = refs[2 * count + 3 : 3 * count + 3]
    gain_out, w_out, w, wide, tall, sem = refs[3 * count + 3 :]
    fetch = pltpu.make_async_copy(w_hbm, w, sem)
    fetch.start()
    atoms = atom_h.shape[0]
    me = lax.axis_index("wide")
    starts = [pl.multiple_of(where(me) * feats, feats) for where in order]
    for want, hot, old in zip(wanted, hots, olds):
        chosen = one_hot(want[...] - place("narrow", atoms), atoms)
        hot[...] = chosen
        old[...] = dot(chosen, atom_h[...]).astype(BF16)
    tall[...] = jnp.broadcast_to(gain[...], (tall.shape[1], gain.shape[1])).T
    blocks = [tall[pl.ds(at, feats), :] for at in starts]
    gain_out[...] = jnp.concatenate(blocks, axis=0).T[:8]
    fetch.wait()
    wide[...] = w[...].astype(F32)
    blocks = [wide[pl.ds(at, feats), :] for at in starts]
    w_out[...] = jnp.concatenate(blocks, axis=0).astype(BF16)


def sum_kernel(count, later, received, *refs):
    quarters, outs, total = refs[:count], refs[count + later : -1], refs[-1]
    _, rows, lanes = received.shape
    half = rows - 8
    edges = quarters[0].shape[1]
    parts = edges // lanes
    me = lax.axis_index("wide")
    ids = iota((total.shape[1], lanes), 0).astype(F32)
    value = jnp.zeros(total.shape, F32)
    for q, quarter in enumerate(quarters):
        codes = received[pl.ds(me ^ q, 1), half:, :].reshape(rows - half, lanes).astype(F32)
        hot = [
            jnp.where(ids == codes[i : i + 1] * 256.0 + codes[parts + i : parts + i + 1], 1.0, 0.0)
            for i in range(parts)
        ]
        value += dot_nt(quarter[...], jnp.concatenate(hot, axis=1).astype(BF16))
    total[...] = value
    feats = total.shape[0] // len(outs)
    for k, out in enumerate(outs):
        at = pl.multiple_of((me // count ^ k) * feats, feats)
        out[...] = total[pl.ds(at, feats), :].astype(out.dtype)


def add_kernel(count, *refs):
    value = refs[0][...]
    for r in refs[1:count]:
        value = value + r[...].astype(F32)
    refs[-1][...] = value.astype(BF16)


def stacked(pieces):
    return jnp.concatenate([p[...] for p in pieces], axis=0)


def updated(hot, table, gain, w_atom, old):
    rows = dot_nt(hot, table)
    scale = lax.rsqrt(jnp.mean(rows * rows, axis=-1, keepdims=True) + 1e-06)
    normed = (rows * scale * gain).astype(BF16)
    return (old.astype(F32) + silu(dot(normed, w_atom))).astype(BF16)


def asked_kernel(count, *refs):
    sent = refs[len(refs) - count :]
    hots, olds = refs[:count], refs[count : 2 * count]
    gain, w_atom = refs[2 * count : 2 * count + 2]
    table = stacked(refs[2 * count + 2 : len(refs) - count])
    for hot, old, send in zip(hots, olds, sent):
        send[...] = updated(hot[...], table, gain[:1, :], w_atom[...], old[...])


def local_kernel(gain, w_atom, atom_h, source, target, w_src, w_tgt, *refs):
    *pieces, atom_hbm, out, atom_out, sem = refs
    atoms = atom_h.shape[0]
    first = place("narrow", atoms)
    same = iota((atoms, atoms), 0) == iota((atoms, atoms), 1)
    same = jnp.where(same, 1.0, 0.0).astype(BF16)
    rows = updated(same, stacked(pieces), gain[:1, :], w_atom[...], atom_h[...])
    atom_out[...] = rows
    store = pltpu.make_async_copy(atom_out, atom_hbm, sem)
    store.start()
    sources = dot(one_hot(source[...] - first, atoms), rows).astype(BF16)
    targets = dot(one_hot(target[...] - first, atoms), rows).astype(BF16)
    out[...] = dot(sources, w_src[...]) + dot(targets, w_tgt[...])
    store.wait()


def final_kernel(count, *refs):
    partial, mid, w_src = refs[:3]
    rows = refs[3 : 3 + count]
    out_hbm, out, sems = refs[3 + count :]
    got = None
    if rows:
        got = rows[0][...].astype(F32)
        for r in rows[1:]:
            got = got + r[...].astype(F32)
        got = got.astype(BF16)
    chunks = sems.shape[0]
    step = out.shape[1] // chunks
    stores = []
    for c in range(chunks):
        part = slice(c * step, (c + 1) * step)
        update = partial[:, part]
        if rows:
            update = update + dot(got, w_src[:, part])
        out[:, part] = (mid[:, part].astype(F32) + silu(update)).astype(BF16)
        at = pl.ds(c * step, step)
        stores.append(pltpu.make_async_copy(out.at[:, at], out_hbm.at[:, at], sems.at[c]))
        stores[-1].start()
    for store in stores:
        store.wait()


def stage_factors(wide):
    stages = []
    left = wide
    size = min(4, max(1, wide // 4))
    stride = wide
    for f in (size, max(1, wide // (2 * size)), 2):
        if f > 1 and left % f == 0:
            stride //= f
            left //= f
            stages.append((stride, f))
    return stages


def gathered(share, wide, feats):
    groups = [(share, [lambda me: me])]
    stages = stage_factors(wide)
    for number, (stride, size) in enumerate(stages):
        mirror = size & (size - 1) == 0

        def turned(at, k, size=size, mirror=mirror):
            return at ^ k if mirror else (at + k) % size

        def moved(k, stride=stride, size=size, turned=turned, mirror=mirror):
            def owner(me):
                at = (me // stride) % size
                return me + (turned(at, k if mirror else size - k) - at) * stride
            return owner

        fresh = []
        for value, owners in groups:
            got = [(value, owners)]
            for k in range(1, size):
                pairs = []
                for i in range(wide):
                    at = (i // stride) % size
                    pairs.append((i, i + (turned(at, k) - at) * stride))
                back = moved(k)
                got.append(
                    (
                        value if value is None else lax.ppermute(value, "wide", pairs),
                        [lambda me, o=o, back=back: o(back(me)) for o in owners],
                    )
                )
            if size > 2:
                fresh.append(
                    (
                        None if value is None else jnp.concatenate([v for v, _ in got], axis=0),
                        [o for _, os in got for o in os],
                    )
                )
            else:
                fresh.extend(got)
        groups = fresh
    return groups


def per_device(
    wide,
    narrow,
    edge_msg,
    basis,
    atom_h,
    edge_source,
    edge_target,
    send_rows,
    trip_slot,
    w_down,
    w_bil,
    w_up,
    w_atom_in,
    atom_gain,
    w_atom,
    w_src,
    w_tgt,
):
    edges, de = edge_msg.shape
    width = w_down.shape[1]
    basis_count = w_bil.shape[0] // width
    triplets = trip_slot.shape[1]
    atoms, da = atom_h.shape
    slots = send_rows.shape[1]
    cap = slots // wide
    feats = da // wide
    lanes = 2 * width
    low = min(4, wide)
    high = wide // low
    big = (24 << 20) if slots <= 512 else (60 << 20)
    shape = jax.ShapeDtypeStruct

    source = edge_source.reshape(1, edges)
    target = edge_target.reshape(1, edges)
    dma = pltpu.SemaphoreType.DMA

    outgoing = call(
        functools.partial(outgoing_kernel, atoms),
        [HBM] * 4,
        VMEM,
        shape((wide, cap // 2 + 8, lanes), BF16),
        big,
        scratch=[
            pltpu.VMEM((edges, de), BF16),
            pltpu.VMEM((width, de), BF16),
            pltpu.VMEM((1, slots), jnp.int32),
            pltpu.VMEM((1, edges), jnp.int32),
            dma((5,)),
        ],
        name="outgoing",
    )(edge_msg, w_down.T, send_rows, target)
    received = lax.all_to_all(outgoing, "wide", split_axis=0, concat_axis=0, tiled=True)

    per = 256 // triplets
    kept = max(1, min(basis_count - 1, (3 << 20) // (edges * slots * 2)))
    rest_shape = (basis_count - kept, edges, slots)
    mixer = call(
        functools.partial(mixer_kernel, cap),
        [HBM, HBM],
        [VMEM, HBM],
        [shape((kept, edges, slots), BF16), shape(rest_shape, BF16)],
        big,
        scratch=[
            pltpu.VMEM(basis.shape, BF16),
            pltpu.VMEM((triplets, edges), jnp.int32),
            pltpu.VMEM((edges // per, per * triplets), jnp.int32),
            pltpu.VMEM(basis.shape, F32),
            pltpu.VMEM(rest_shape, BF16),
            dma((6,)),
        ],
        cost=cost(2 * basis_count * edges * slots * 256, 6 << 20),
        name="mixer",
    )(basis, trip_slot.T)

    edge_mid, *quarters = call(
        edge_kernel,
        [VMEM] * 2 + [HBM] * 5,
        [HBM] + [VMEM] * low,
        [shape((edges, de), BF16)] + [shape((feats * high, edges), BF16)] * low,
        big,
        scratch=[
            pltpu.VMEM(rest_shape, BF16),
            pltpu.VMEM((edges, de), BF16),
            pltpu.VMEM((width, basis_count * width), BF16),
            pltpu.VMEM(w_up.shape, BF16),
            pltpu.VMEM(w_atom_in.shape, BF16),
            pltpu.VMEM((edges, de), BF16),
            pltpu.VMEM((da, edges), F32),
            dma((6,)),
        ],
        name="edge",
    )(received, *mixer, edge_msg, w_bil.T, w_up, w_atom_in)
    def mirrored(value, flip):
        return lax.ppermute(value, "wide", [(i, i ^ flip) for i in range(wide)])

    quarters = quarters[:1] + [mirrored(v, q) for q, v in enumerate(quarters) if q]
    source_late, quarters[1] = lax.optimization_barrier((source, quarters[1]))
    wanted = [
        lax.ppermute(source_late, "narrow", [(i, (i + k) % narrow) for i in range(narrow)])
        for k in range(1, narrow)
    ]
    def block(owner):
        return lambda me: owner(me) % low * high + owner(me) // low

    order = [block(o) for _, os in gathered(None, wide, feats) for o in os]
    *picks, gain_near, w_atom_near = call(
        functools.partial(picks_kernel, order, feats, len(wanted)),
        [VMEM] * (len(wanted) + 2) + [HBM],
        [VMEM] * (2 * len(wanted) + 2),
        [shape((edges, atoms), BF16)] * len(wanted)
        + [shape((edges, da), BF16)] * len(wanted)
        + [shape((8, da), F32), shape(w_atom.shape, BF16)],
        big,
        scratch=[
            pltpu.VMEM(w_atom.shape, BF16),
            pltpu.VMEM(w_atom.shape, F32),
            pltpu.VMEM((da, 128), F32),
            dma,
        ],
        cost=cost(1 << 26, 2 << 20),
        name="picks",
    )(*wanted, atom_h, atom_gain.reshape(1, da), w_atom)
    sums = call(
        functools.partial(sum_kernel, low, len(wanted)),
        [VMEM] * (1 + low) + [pl.BlockSpec(memory_space=pl.ANY)] * len(wanted),
        [VMEM] * high,
        [shape((feats, atoms), F32)] + [shape((feats, atoms), BF16)] * (high - 1),
        big,
        scratch=[pltpu.VMEM((feats * high, atoms), F32)],
        name="sums",
    )(received, *quarters, *wanted)
    far = [mirrored(sums[k], k * low) for k in range(high - 1, 0, -1)]
    sums = [sums[0]] + far[::-1]
    share = call(
        functools.partial(add_kernel, high),
        [VMEM] * high + [pl.BlockSpec(memory_space=pl.ANY)] * len(picks),
        VMEM,
        shape((feats, atoms), BF16),
        big,
        name="add",
    )(*sums, *picks)

    pieces = [v for v, _ in gathered(share, wide, feats)]
    asked = call(
        functools.partial(asked_kernel, len(wanted)),
        [VMEM] * (len(picks) + 2 + len(pieces)),
        [VMEM] * len(wanted),
        [shape((edges, da), BF16)] * len(wanted),
        big,
        name="asked",
    )(*picks, gain_near, w_atom_near, *pieces)
    rows = [
        lax.ppermute(a, "narrow", [(i, (i - k) % narrow) for i in range(narrow)])
        for k, a in enumerate(asked, start=1)
    ]
    atom_out, partial = call(
        local_kernel,
        [VMEM] * (7 + len(pieces)),
        [HBM, VMEM],
        (shape((atoms, da), BF16), shape((edges, de), F32)),
        big,
        scratch=[pltpu.VMEM((atoms, da), BF16), dma],
        cost=cost(4 * edges * da * de + 8 * edges * da * atoms, 4 << 20),
        name="local",
    )(gain_near, w_atom_near, atom_h, source, target, w_src, w_tgt, *pieces)
    edge_out = call(
        functools.partial(final_kernel, len(rows)),
        [VMEM] * (3 + len(rows)),
        HBM,
        shape((edges, de), BF16),
        big,
        scratch=[pltpu.VMEM((edges, de), BF16), dma((4,))],
        name="final",
    )(partial, edge_mid, w_src, *rows)
    return (edge_out, atom_out)


def solution(mesh):
    placed = (
        P(("wide", "narrow"), None),
        P(("wide", "narrow"), None),
        P("narrow", None),
        P(("wide", "narrow")),
        P(("wide", "narrow")),
        P(("wide", "narrow"), None),
        P(("wide", "narrow"), None),
        P(),
        P(),
        P(),
        P(),
        P(),
        P(),
        P(),
        P(),
    )
    return jax.shard_map(
        functools.partial(per_device, mesh.shape["wide"], mesh.shape["narrow"]),
        mesh=mesh,
        in_specs=placed,
        out_specs=(P(("wide", "narrow"), None), P("narrow", None)),
        check_vma=False,
    )
```

```python
import functools

import jax
import jax.numpy as jnp
from jax import lax
from jax.experimental import pallas as pl
from jax.experimental.pallas import tpu as pltpu
from jax.sharding import PartitionSpec as P

F32 = jnp.float32
BF16 = jnp.bfloat16
NT = (((1,), (1,)), ((), ()))


def silu(value):
    return value / (1.0 + jnp.exp(-value))


def dot(a, b):
    return jnp.dot(a, b, preferred_element_type=F32)


def dot_nt(a, b):
    return lax.dot_general(a, b, NT, preferred_element_type=F32)


def iota(shape, dim):
    return lax.broadcasted_iota(jnp.int32, shape, dim)


def column(row):
    return jnp.broadcast_to(row, (8, row.shape[1])).T[:, :1]


VMEM = pl.BlockSpec(memory_space=pltpu.VMEM)
HBM = pl.BlockSpec(memory_space=pltpu.HBM)


def quotient(value, by):
    if by & (by - 1) == 0:
        return lax.shift_right_logical(value, by.bit_length() - 1)
    return lax.div(value, jnp.int32(by))


def remainder(value, by):
    if by & (by - 1) == 0:
        return lax.bitwise_and(value, by - 1)
    return lax.rem(value, jnp.int32(by))


def call(kernel, ins, outs, out_shape, vmem, scratch=(), cost=None, name=None, alias=()):
    def kept(spec, leaf):
        return pltpu.HBM(leaf.shape, leaf.dtype) if spec is HBM else leaf

    many = isinstance(out_shape, (list, tuple))
    out_shape = [kept(o, s) for o, s in zip(outs, out_shape)] if many else kept(outs, out_shape)
    run = pl.pallas_call(
        kernel,
        out_shape=out_shape,
        in_specs=list(ins),
        out_specs=outs,
        scratch_shapes=list(scratch),
        input_output_aliases=dict(alias),
        compiler_params=pltpu.CompilerParams(vmem_limit_bytes=vmem),
        cost_estimate=cost,
        name=name,
    )

    def apply(*args):
        held = [
            pltpu.with_memory_space_constraint(a, pltpu.HBM) if spec is HBM else a
            for spec, a in zip(ins, args)
        ]
        return run(*held)

    return apply


def cost(flops, moved):
    return pl.CostEstimate(flops=int(flops), bytes_accessed=int(moved), transcendentals=0)


def place(axis, size):
    return lax.axis_index(axis) * size


def one_hot(index, count):
    hot = column(index) == iota((index.shape[1], count), 1)
    return jnp.where(hot, 1.0, 0.0).astype(BF16)


def outgoing_kernel(
    edge_hbm,
    w_hbm,
    rows_hbm,
    basis_hbm,
    slots_hbm,
    out,
    basis,
    slots_t,
    edge,
    w,
    rows,
    sems,
):
    edges = edge.shape[0]
    width = w.shape[0]
    peers, half, lanes = out.shape
    slots = peers * half * 2
    chunks = sems.shape[0] - 4
    step = edges // chunks
    copies = [
        pltpu.make_async_copy(rows_hbm, rows, sems.at[0]),
        pltpu.make_async_copy(w_hbm, w, sems.at[1]),
    ]
    for i in range(chunks):
        part = pl.ds(i * step, step)
        copies.append(pltpu.make_async_copy(edge_hbm.at[part, :], edge.at[part, :], sems.at[2 + i]))
    extra = [
        pltpu.make_async_copy(slots_hbm, slots_t, sems.at[2 + chunks]),
        pltpu.make_async_copy(basis_hbm, basis, sems.at[3 + chunks]),
    ]
    for c in copies + extra:
        c.start()
    copies[0].wait()
    hot = one_hot(rows[...], edges)
    copies[1].wait()
    down_w = w[...]
    twice = jnp.concatenate([down_w, down_w], axis=0)
    down = []
    for i in range(chunks):
        copies[2 + i].wait()
        down.append(silu(dot_nt(edge[i * step : (i + 1) * step, :], twice)).astype(BF16))
    picked = dot(hot, jnp.concatenate(down, axis=0))
    picked = picked.reshape(peers, 2 * half, lanes)
    low = iota((peers, half, lanes), 2) < width
    packed = jnp.where(low, picked[:, :half], picked[:, half:])
    out[...] = packed.astype(BF16)
    for c in extra:
        c.wait()


def start_first(copies):
    def go(_, carry):
        for c in copies:
            c.start()
        return carry

    lax.fori_loop(0, jnp.minimum(lax.axis_index("wide"), 0) + 1, go, 0)


def mixer_kernel(
    cap, basis, slots_t, kept, rest_hbm, flat, spread, rest, sems
):
    kept_count, edges, slots = kept.shape
    basis_count = kept_count + rest_hbm.shape[0]
    triplets = slots_t.shape[0]
    groups, span = flat.shape
    per = edges // groups
    total = basis.shape[1]
    rows, cols = iota((total, total), 0), iota((total, total), 1)
    order = quotient(rows, basis_count) + remainder(rows, basis_count) * triplets == cols
    order = jnp.where(order, 1.0, 0.0).astype(BF16)
    own = remainder(iota((edges, span), 0), per) == quotient(iota((edges, span), 1), triplets)
    half = cap // 2
    slot = slots_t[...]
    slot = (
        remainder(quotient(slot, half), 2) * (slots // 2)
        + quotient(slot, cap) * half
        + remainder(slot, half)
    )
    slot = slot.T
    turn = remainder(iota((triplets, span), 1), triplets)
    tile = jnp.where(iota((triplets, span), 0) == turn, 1.0, 0.0)
    tile = tile.astype(BF16)
    high = lax.shift_right_logical(slot, 8).astype(F32).astype(BF16)
    low = lax.bitwise_and(slot, 255).astype(F32).astype(BF16)
    wide = jnp.where(own, dot(high, tile) * 256.0 + dot(low, tile), 0.0)
    flat[...] = jnp.sum(wide.reshape(groups, per, span), axis=1).astype(jnp.int32)
    by_basis = dot(basis[...], order)
    pack = 128 // triplets
    turn = remainder(iota((edges, 128), 0), pack)
    for q in range(total // 128):
        lanes = by_basis[:, q * 128 : (q + 1) * 128]
        turned = lanes
        for r in range(1, pack):
            turned = jnp.where(turn == r, pltpu.roll(lanes, r * triplets, 1), turned)
        spread[:, q * 128 : (q + 1) * 128] = turned
    row, lane = iota((per, 128), 0), quotient(iota((per, 128), 1), triplets)
    mine = [row == lane + c * pack for c in range(span // 128)]

    def one(pair):
        parts = []
        for h in range(2):
            group = pair * 2 + h
            values = spread[pl.ds(pl.multiple_of(group * per, per), per), :]
            left = []
            for k in range(basis_count):
                q, j = k // pack, k % pack
                lanes = values[:, q * 128 : (q + 1) * 128]
                if j:
                    lanes = pltpu.roll(lanes, 128 - j * triplets, 1)
                left.append(jnp.concatenate([jnp.where(m, lanes, 0.0) for m in mine], axis=1))
            left = jnp.concatenate(left, axis=0).astype(BF16)
            hot = iota((slots, span), 0) == flat[pl.ds(group, 1), :]
            part = dot_nt(left, jnp.where(hot, 1.0, 0.0).astype(BF16))
            parts.append(part.reshape(basis_count, per, slots))
        both = jnp.concatenate(parts, axis=1).astype(BF16)
        at = pl.ds(pl.multiple_of(pair * 2 * per, 2 * per), 2 * per)
        kept[:, at, :] = both[:kept_count]
        rest[:, at, :] = both[kept_count:]

    unroll = 4

    def step(i, _):
        for u in range(unroll):
            one(unroll * i + u)
        return 0

    chunks = sems.shape[0]
    steps = groups // 2 // unroll // chunks
    copies = []
    for c in range(chunks):
        lax.fori_loop(c * steps, (c + 1) * steps, step, 0)
        size = steps * unroll * 2 * per
        part = pl.ds(c * size, size)
        copies.append(
            pltpu.make_async_copy(rest.at[:, part, :], rest_hbm.at[:, part, :], sems.at[c])
        )
        copies[-1].start()
    for c in copies:
        c.wait()


def edge_kernel(
    atoms,
    received,
    target,
    kept,
    rest_hbm,
    edge_hbm,
    w_bil_hbm,
    w_up_hbm,
    w_atom_hbm,
    mid_hbm,
    *refs,
):
    *quarters, rest, edge_msg, w_bil_t, w_up, w_atom_in, edge_mid, message, sems = refs
    peers, half, lanes = received.shape
    width = w_bil_t.shape[0]
    pairs = [
        (rest_hbm, rest),
        (w_bil_hbm, w_bil_t),
        (w_up_hbm, w_up),
        (edge_hbm, edge_msg),
        (w_atom_hbm, w_atom_in),
    ]
    copies = [pltpu.make_async_copy(a, b, sems.at[i]) for i, (a, b) in enumerate(pairs)]
    start_first(copies)
    got = received[...].astype(F32).reshape(peers * half, lanes).T
    table = jnp.concatenate([got[:width], got[width:]], axis=1).astype(BF16)
    mixed = [dot_nt(table, kept[k]).astype(BF16) for k in range(kept.shape[0])]
    copies[0].wait()
    mixed += [dot_nt(table, rest[k]).astype(BF16) for k in range(rest.shape[0])]
    mixed = jnp.concatenate(mixed, axis=0)
    copies[1].wait()
    trip = silu(dot(w_bil_t[...], mixed)).T.astype(BF16)
    copies[2].wait()
    copies[3].wait()
    mid = (edge_msg[...].astype(F32) + dot(trip, w_up[...])).astype(BF16)
    edge_mid[...] = mid
    store = pltpu.make_async_copy(edge_mid, mid_hbm, sems.at[len(pairs)])
    store.start()
    local = target[...] - place("narrow", atoms)
    codes = [lax.shift_right_logical(local, 8), lax.bitwise_and(local, 255)]
    codes += [jnp.zeros_like(local)] * 14
    codes = jnp.concatenate(codes, axis=0).astype(F32).astype(BF16)
    copies[4].wait()
    message[...] = dot(mid, w_atom_in[...]).T.astype(BF16)
    part = message.shape[0] // len(quarters)
    mine = lax.axis_index("wide") % len(quarters)
    for q, quarter in enumerate(quarters):
        at = pl.multiple_of((mine ^ q) * part, part)
        quarter[:part, :] = message[pl.ds(at, part), :]
        quarter[part:, :] = codes
    store.wait()


def picks_kernel(order, feats, count, *refs):
    wanted = refs[:count]
    atom_h, gain, w_hbm = refs[count : count + 3]
    *given, gain_out, w_out, w, wide, tall, sem = refs[count + 3 :]
    fetch = pltpu.make_async_copy(w_hbm, w, sem)
    fetch.start()
    atoms = atom_h.shape[0]
    me = lax.axis_index("wide")
    starts = [pl.multiple_of(where(me) * feats, feats) for where in order]
    for i, want in enumerate(wanted):
        chosen = one_hot(want[...] - place("narrow", atoms), atoms)
        value = dot(chosen, atom_h[...]).astype(BF16)
        at = 0
        for hot, old in zip(given[2 * i :: 2 * count], given[2 * i + 1 :: 2 * count]):
            size = hot.shape[0]
            hot[...] = chosen[at : at + size]
            old[...] = value[at : at + size]
            at += size
    tall[...] = jnp.broadcast_to(gain[...], (tall.shape[1], gain.shape[1])).T
    blocks = [tall[pl.ds(at, feats), :] for at in starts]
    gain_out[...] = jnp.concatenate(blocks, axis=0).T[:8]
    fetch.wait()
    wide[...] = w[...].astype(F32)
    blocks = [wide[pl.ds(at, feats), :] for at in starts]
    w_out[...] = jnp.concatenate(blocks, axis=0).astype(BF16)


def sum_kernel(count, later, *refs):
    quarters, outs, total = refs[:count], refs[count + later : -1], refs[-1]
    me = lax.axis_index("wide")
    part, atoms = total.shape
    ids = iota((atoms, quarters[0].shape[1]), 0).astype(F32)
    value = jnp.zeros(total.shape, F32)
    for quarter in quarters:
        codes = quarter[part:, :].astype(F32)
        hot = jnp.where(ids == codes[0:1] * 256.0 + codes[1:2], 1.0, 0.0)
        value += dot_nt(quarter[:part, :], hot.astype(BF16))
    total[...] = value
    feats = total.shape[0] // len(outs)
    for i, out in enumerate(outs):
        k = -i % len(outs)
        at = pl.multiple_of((me // count ^ k) * feats, feats)
        out[...] = total[pl.ds(at, feats), :].astype(out.dtype)


def add_kernel(count, *refs):
    value = refs[0][...]
    for r in refs[1:count]:
        value = value + r[...].astype(F32)
    refs[-1][...] = value.astype(BF16)


def stacked(pieces):
    return jnp.concatenate([p[...] for p in pieces], axis=0)


def updated(hot, table, gain, w_atom, old):
    rows = dot_nt(hot, table)
    scale = lax.rsqrt(jnp.mean(rows * rows, axis=-1, keepdims=True) + 1e-06)
    normed = (rows * scale * gain).astype(BF16)
    return (old.astype(F32) + silu(dot(normed, w_atom))).astype(BF16)


def asked_kernel(count, *refs):
    sent = refs[len(refs) - count :]
    hots, olds = refs[: 2 * count : 2], refs[1 : 2 * count : 2]
    gain, w_atom = refs[2 * count : 2 * count + 2]
    table = stacked(refs[2 * count + 2 : len(refs) - count])
    for hot, old, send in zip(hots, olds, sent):
        send[...] = updated(hot[...], table, gain[:1, :], w_atom[...], old[...])


def local_kernel(gain, w_atom, atom_h, source, target, w_src, w_tgt, *refs):
    *pieces, atom_hbm, out, atom_out, sem = refs
    atoms = atom_h.shape[0]
    first = place("narrow", atoms)
    same = iota((atoms, atoms), 0) == iota((atoms, atoms), 1)
    same = jnp.where(same, 1.0, 0.0).astype(BF16)
    rows = updated(same, stacked(pieces), gain[:1, :], w_atom[...], atom_h[...])
    atom_out[...] = rows
    store = pltpu.make_async_copy(atom_out, atom_hbm, sem)
    store.start()
    sources = dot(one_hot(source[...] - first, atoms), rows).astype(BF16)
    targets = dot(one_hot(target[...] - first, atoms), rows).astype(BF16)
    out[...] = dot(sources, w_src[...]) + dot(targets, w_tgt[...])
    store.wait()


def final_kernel(count, start, *refs):
    partial, mid, w_src = refs[:3]
    rows = refs[3 : 3 + count]
    out_hbm, out, sems = refs[-3:]
    size = out.shape[0]
    these = slice(start, start + size)
    got = rows[0][...].astype(F32)
    for r in rows[1:]:
        got = got + r[...].astype(F32)
    got = got.astype(BF16)
    chunks = sems.shape[0]
    step = out.shape[1] // chunks
    stores = []
    for c in range(chunks):
        part = slice(c * step, (c + 1) * step)
        update = partial[these, part] + dot(got, w_src[:, part])
        out[:, part] = (mid[these, part].astype(F32) + silu(update)).astype(BF16)
        at = pl.ds(c * step, step)
        to = out_hbm.at[pl.ds(start, size), at]
        stores.append(pltpu.make_async_copy(out.at[:, at], to, sems.at[c]))
        stores[-1].start()
    for store in stores:
        store.wait()


def stage_factors(wide):
    stages = []
    left = wide
    size = min(4, max(1, wide // 4))
    stride = wide
    for f in (size, max(1, wide // (2 * size)), 2):
        if f > 1 and left % f == 0:
            stride //= f
            left //= f
            stages.append((stride, f))
    return stages


def gathered(share, wide, feats):
    groups = [(share, [lambda me: me])]
    stages = stage_factors(wide)
    for number, (stride, size) in enumerate(stages):
        mirror = size & (size - 1) == 0

        def turned(at, k, size=size, mirror=mirror):
            return at ^ k if mirror else (at + k) % size

        def moved(k, stride=stride, size=size, turned=turned, mirror=mirror):
            def owner(me):
                at = (me // stride) % size
                return me + (turned(at, k if mirror else size - k) - at) * stride
            return owner

        fresh = []
        for value, owners in groups:
            got = [(value, owners)]
            for k in range(1, size):
                pairs = []
                for i in range(wide):
                    at = (i // stride) % size
                    pairs.append((i, i + (turned(at, k) - at) * stride))
                back = moved(k)
                got.append(
                    (
                        value if value is None else lax.ppermute(value, "wide", pairs),
                        [lambda me, o=o, back=back: o(back(me)) for o in owners],
                    )
                )
            if size > 2:
                fresh.append(
                    (
                        None if value is None else jnp.concatenate([v for v, _ in got], axis=0),
                        [o for _, os in got for o in os],
                    )
                )
            else:
                fresh.extend(got)
        groups = fresh
    return groups


def per_device(
    wide,
    narrow,
    edge_msg,
    basis,
    atom_h,
    edge_source,
    edge_target,
    send_rows,
    trip_slot,
    w_down,
    w_bil,
    w_up,
    w_atom_in,
    atom_gain,
    w_atom,
    w_src,
    w_tgt,
):
    edges, de = edge_msg.shape
    width = w_down.shape[1]
    basis_count = w_bil.shape[0] // width
    triplets = trip_slot.shape[1]
    atoms, da = atom_h.shape
    slots = send_rows.shape[1]
    cap = slots // wide
    feats = da // wide
    lanes = 2 * width
    bounds = [0, edges // 2, edges]
    sizes = [b - a for a, b in zip(bounds, bounds[1:])]
    low = min(4, wide)
    high = wide // low
    big = (24 << 20) if slots <= 512 else (60 << 20)
    shape = jax.ShapeDtypeStruct

    source = edge_source.reshape(1, edges)
    target = edge_target.reshape(1, edges)
    dma = pltpu.SemaphoreType.DMA

    outgoing, basis_near, slots_near = call(
        outgoing_kernel,
        [HBM] * 5,
        [VMEM] * 3,
        [
            shape((wide, cap // 2, lanes), BF16),
            shape(basis.shape, BF16),
            shape((triplets, edges), jnp.int32),
        ],
        big,
        scratch=[
            pltpu.VMEM((edges, de), BF16),
            pltpu.VMEM((width, de), BF16),
            pltpu.VMEM((1, slots), jnp.int32),
            dma((6,)),
        ],
        name="outgoing",
    )(edge_msg, w_down.T, send_rows, basis, trip_slot.T)
    received = lax.all_to_all(outgoing, "wide", split_axis=0, concat_axis=0, tiled=True)

    per = 256 // triplets
    kept = max(1, min(basis_count - 1, (3 << 20) // (edges * slots * 2)))
    rest_shape = (basis_count - kept, edges, slots)
    mixer = call(
        functools.partial(mixer_kernel, cap),
        [VMEM, VMEM],
        [VMEM, HBM],
        [shape((kept, edges, slots), BF16), shape(rest_shape, BF16)],
        big,
        scratch=[
            pltpu.VMEM((edges // per, per * triplets), jnp.int32),
            pltpu.VMEM(basis.shape, F32),
            pltpu.VMEM(rest_shape, BF16),
            dma((4,)),
        ],
        cost=cost(2 * basis_count * edges * slots * 256, 6 << 20),
        name="mixer",
    )(basis_near, slots_near)

    edge_mid, *quarters = call(
        functools.partial(edge_kernel, atoms),
        [VMEM] * 3 + [HBM] * 5,
        [HBM] + [VMEM] * low,
        [shape((edges, de), BF16)] + [shape((feats * high + 16, edges), BF16)] * low,
        big,
        scratch=[
            pltpu.VMEM(rest_shape, BF16),
            pltpu.VMEM((edges, de), BF16),
            pltpu.VMEM((width, basis_count * width), BF16),
            pltpu.VMEM(w_up.shape, BF16),
            pltpu.VMEM(w_atom_in.shape, BF16),
            pltpu.VMEM((edges, de), BF16),
            pltpu.VMEM((da, edges), BF16),
            dma((6,)),
        ],
        name="edge",
    )(received, target, *mixer, edge_msg, w_bil.T, w_up, w_atom_in)
    def mirrored(value, flip):
        return lax.ppermute(value, "wide", [(i, i ^ flip) for i in range(wide)])

    quarters = quarters[:1] + [mirrored(v, q) for q, v in enumerate(quarters) if q]
    source_late, quarters[1] = lax.optimization_barrier((source, quarters[1]))
    wanted = [
        lax.ppermute(source_late, "narrow", [(i, (i + k) % narrow) for i in range(narrow)])
        for k in range(1, narrow)
    ]
    def block(owner):
        return lambda me: owner(me) % low * high + owner(me) // low

    order = [block(o) for _, os in gathered(None, wide, feats) for o in os]
    *picks, gain_near, w_atom_near = call(
        functools.partial(picks_kernel, order, feats, len(wanted)),
        [VMEM] * (len(wanted) + 2) + [HBM],
        [VMEM] * (2 * len(sizes) * len(wanted) + 2),
        [shape((n, w), BF16) for n in sizes for _ in wanted for w in (atoms, da)]
        + [shape((8, da), F32), shape(w_atom.shape, BF16)],
        big,
        scratch=[
            pltpu.VMEM(w_atom.shape, BF16),
            pltpu.VMEM(w_atom.shape, F32),
            pltpu.VMEM((da, 128), F32),
            dma,
        ],
        cost=cost(1 << 26, 2 << 20),
        name="picks",
    )(*wanted, atom_h, atom_gain.reshape(1, da), w_atom)
    sums = call(
        functools.partial(sum_kernel, low, len(wanted)),
        [VMEM] * low + [pl.BlockSpec(memory_space=pl.ANY)] * len(wanted),
        [VMEM] * high,
        [shape((feats, atoms), F32)] + [shape((feats, atoms), BF16)] * (high - 1),
        big,
        scratch=[pltpu.VMEM((feats * high, atoms), F32)],
        name="sums",
    )(*quarters, *wanted)
    sums = [sums[0]] + [mirrored(v, -i % high * low) for i, v in enumerate(sums) if i]
    share = call(
        functools.partial(add_kernel, high),
        [VMEM] * high + [pl.BlockSpec(memory_space=pl.ANY)] * len(picks),
        VMEM,
        shape((feats, atoms), BF16),
        big,
        name="add",
    )(*sums, *picks)

    pieces = [v for v, _ in gathered(share, wide, feats)]
    rows = []
    for h, size in enumerate(sizes):
        given = picks[2 * len(wanted) * h : 2 * len(wanted) * (h + 1)]
        asked = call(
            functools.partial(asked_kernel, len(wanted)),
            [VMEM] * (len(given) + 2 + len(pieces)),
            [VMEM] * len(wanted),
            [shape((size, da), BF16)] * len(wanted),
            big,
            name=f"asked{h}",
        )(*given, gain_near, w_atom_near, *pieces)
        rows.append(
            [
                lax.ppermute(a, "narrow", [(i, (i - k) % narrow) for i in range(narrow)])
                for k, a in enumerate(asked, start=1)
            ]
        )
    atom_out, partial = call(
        local_kernel,
        [VMEM] * (7 + len(pieces)),
        [HBM, VMEM],
        (shape((atoms, da), BF16), shape((edges, de), F32)),
        big,
        scratch=[pltpu.VMEM((atoms, da), BF16), dma],
        cost=cost(4 * edges * da * de + 8 * edges * da * atoms, 4 << 20),
        name="local",
    )(gain_near, w_atom_near, atom_h, source, target, w_src, w_tgt, *pieces)
    edge_out = []
    for h, got in enumerate(rows):
        held = 3 + len(got) + len(edge_out)
        edge_out = [
            call(
                functools.partial(final_kernel, len(got), bounds[h]),
                [VMEM] * (3 + len(got)) + [HBM] * len(edge_out),
                HBM,
                shape((edges, de), BF16),
                big,
                scratch=[pltpu.VMEM((sizes[h], de), BF16), dma((2,))],
                name=f"final{h}",
                alias={held - 1: 0} if edge_out else {},
            )(partial, edge_mid, w_src, *got, *edge_out)
        ]
    edge_out = edge_out[0]
    return (edge_out, atom_out)


def solution(mesh):
    placed = (
        P(("wide", "narrow"), None),
        P(("wide", "narrow"), None),
        P("narrow", None),
        P(("wide", "narrow")),
        P(("wide", "narrow")),
        P(("wide", "narrow"), None),
        P(("wide", "narrow"), None),
        P(),
        P(),
        P(),
        P(),
        P(),
        P(),
        P(),
        P(),
    )
    return jax.shard_map(
        functools.partial(per_device, mesh.shape["wide"], mesh.shape["narrow"]),
        mesh=mesh,
        in_specs=placed,
        out_specs=(P(("wide", "narrow"), None), P("narrow", None)),
        check_vma=False,
    )
```

```python
import functools

import jax
import jax.numpy as jnp
from jax import lax
from jax.experimental import pallas as pl
from jax.experimental.pallas import tpu as pltpu
from jax.sharding import PartitionSpec as P

F32 = jnp.float32
BF16 = jnp.bfloat16
NT = (((1,), (1,)), ((), ()))


def silu(value):
    return value / (1.0 + jnp.exp(-value))


def dot(a, b):
    return jnp.dot(a, b, preferred_element_type=F32)


def dot_nt(a, b):
    return lax.dot_general(a, b, NT, preferred_element_type=F32)


def iota(shape, dim):
    return lax.broadcasted_iota(jnp.int32, shape, dim)


def column(row):
    return jnp.broadcast_to(row, (8, row.shape[1])).T[:, :1]


VMEM = pl.BlockSpec(memory_space=pltpu.VMEM)
HBM = pl.BlockSpec(memory_space=pltpu.HBM)


def quotient(value, by):
    if by & (by - 1) == 0:
        return lax.shift_right_logical(value, by.bit_length() - 1)
    return lax.div(value, jnp.int32(by))


def remainder(value, by):
    if by & (by - 1) == 0:
        return lax.bitwise_and(value, by - 1)
    return lax.rem(value, jnp.int32(by))


def call(kernel, ins, outs, out_shape, vmem, scratch=(), cost=None, name=None, alias=()):
    def kept(spec, leaf):
        return pltpu.HBM(leaf.shape, leaf.dtype) if spec is HBM else leaf

    many = isinstance(out_shape, (list, tuple))
    out_shape = [kept(o, s) for o, s in zip(outs, out_shape)] if many else kept(outs, out_shape)
    run = pl.pallas_call(
        kernel,
        out_shape=out_shape,
        in_specs=list(ins),
        out_specs=outs,
        scratch_shapes=list(scratch),
        input_output_aliases=dict(alias),
        compiler_params=pltpu.CompilerParams(vmem_limit_bytes=vmem),
        cost_estimate=cost,
        name=name,
    )

    def apply(*args):
        held = [
            pltpu.with_memory_space_constraint(a, pltpu.HBM) if spec is HBM else a
            for spec, a in zip(ins, args)
        ]
        return run(*held)

    return apply


def cost(flops, moved):
    return pl.CostEstimate(flops=int(flops), bytes_accessed=int(moved), transcendentals=0)


def place(axis, size):
    return lax.axis_index(axis) * size


def one_hot(index, count):
    hot = column(index) == iota((index.shape[1], count), 1)
    return jnp.where(hot, 1.0, 0.0).astype(BF16)


def outgoing_kernel(
    edge_hbm,
    w_hbm,
    rows_hbm,
    basis_hbm,
    slots_hbm,
    out,
    basis,
    slots_t,
    edge,
    w,
    rows,
    sems,
):
    edges = edge.shape[0]
    width = w.shape[0]
    peers, half, lanes = out.shape
    slots = peers * half * 2
    chunks = sems.shape[0] - 4
    step = edges // chunks
    copies = [
        pltpu.make_async_copy(rows_hbm, rows, sems.at[0]),
        pltpu.make_async_copy(w_hbm, w, sems.at[1]),
    ]
    for i in range(chunks):
        part = pl.ds(i * step, step)
        copies.append(pltpu.make_async_copy(edge_hbm.at[part, :], edge.at[part, :], sems.at[2 + i]))
    extra = [
        pltpu.make_async_copy(slots_hbm, slots_t, sems.at[2 + chunks]),
        pltpu.make_async_copy(basis_hbm, basis, sems.at[3 + chunks]),
    ]
    for c in copies + extra:
        c.start()
    copies[0].wait()
    hot = one_hot(rows[...], edges)
    copies[1].wait()
    down_w = w[...]
    twice = jnp.concatenate([down_w, down_w], axis=0)
    down = []
    for i in range(chunks):
        copies[2 + i].wait()
        down.append(silu(dot_nt(edge[i * step : (i + 1) * step, :], twice)).astype(BF16))
    picked = dot(hot, jnp.concatenate(down, axis=0))
    picked = picked.reshape(peers, 2 * half, lanes)
    low = iota((peers, half, lanes), 2) < width
    packed = jnp.where(low, picked[:, :half], picked[:, half:])
    out[...] = packed.astype(BF16)
    for c in extra:
        c.wait()


def start_first(copies):
    def go(_, carry):
        for c in copies:
            c.start()
        return carry

    lax.fori_loop(0, jnp.minimum(lax.axis_index("wide"), 0) + 1, go, 0)


def mixer_kernel(
    cap, basis, slots_t, kept, rest_hbm, flat, spread, rest, sems
):
    kept_count, edges, slots = kept.shape
    basis_count = kept_count + rest_hbm.shape[0]
    triplets = slots_t.shape[0]
    groups, span = flat.shape
    per = edges // groups
    total = basis.shape[1]
    rows, cols = iota((total, total), 0), iota((total, total), 1)
    order = quotient(rows, basis_count) + remainder(rows, basis_count) * triplets == cols
    order = jnp.where(order, 1.0, 0.0).astype(BF16)
    own = remainder(iota((edges, span), 0), per) == quotient(iota((edges, span), 1), triplets)
    half = cap // 2
    slot = slots_t[...]
    slot = (
        remainder(quotient(slot, half), 2) * (slots // 2)
        + quotient(slot, cap) * half
        + remainder(slot, half)
    )
    slot = slot.T
    turn = remainder(iota((triplets, span), 1), triplets)
    tile = jnp.where(iota((triplets, span), 0) == turn, 1.0, 0.0)
    tile = tile.astype(BF16)
    high = lax.shift_right_logical(slot, 8).astype(F32).astype(BF16)
    low = lax.bitwise_and(slot, 255).astype(F32).astype(BF16)
    wide = jnp.where(own, dot(high, tile) * 256.0 + dot(low, tile), 0.0)
    flat[...] = jnp.sum(wide.reshape(groups, per, span), axis=1).astype(jnp.int32)
    by_basis = dot(basis[...], order)
    pack = 128 // triplets
    turn = remainder(iota((edges, 128), 0), pack)
    for q in range(total // 128):
        lanes = by_basis[:, q * 128 : (q + 1) * 128]
        turned = lanes
        for r in range(1, pack):
            turned = jnp.where(turn == r, pltpu.roll(lanes, r * triplets, 1), turned)
        spread[:, q * 128 : (q + 1) * 128] = turned
    row, lane = iota((per, 128), 0), quotient(iota((per, 128), 1), triplets)
    mine = [row == lane + c * pack for c in range(span // 128)]

    def one(pair):
        parts = []
        for h in range(2):
            group = pair * 2 + h
            values = spread[pl.ds(pl.multiple_of(group * per, per), per), :]
            left = []
            for k in range(basis_count):
                q, j = k // pack, k % pack
                lanes = values[:, q * 128 : (q + 1) * 128]
                if j:
                    lanes = pltpu.roll(lanes, 128 - j * triplets, 1)
                left.append(jnp.concatenate([jnp.where(m, lanes, 0.0) for m in mine], axis=1))
            left = jnp.concatenate(left, axis=0).astype(BF16)
            hot = iota((slots, span), 0) == flat[pl.ds(group, 1), :]
            part = dot_nt(left, jnp.where(hot, 1.0, 0.0).astype(BF16))
            parts.append(part.reshape(basis_count, per, slots))
        both = jnp.concatenate(parts, axis=1).astype(BF16)
        at = pl.ds(pl.multiple_of(pair * 2 * per, 2 * per), 2 * per)
        kept[:, at, :] = both[:kept_count]
        rest[:, at, :] = both[kept_count:]

    unroll = 4

    def step(i, _):
        for u in range(unroll):
            one(unroll * i + u)
        return 0

    chunks = sems.shape[0]
    steps = groups // 2 // unroll // chunks
    copies = []
    for c in range(chunks):
        lax.fori_loop(c * steps, (c + 1) * steps, step, 0)
        size = steps * unroll * 2 * per
        part = pl.ds(c * size, size)
        copies.append(
            pltpu.make_async_copy(rest.at[:, part, :], rest_hbm.at[:, part, :], sems.at[c])
        )
        copies[-1].start()
    for c in copies:
        c.wait()


def edge_kernel(
    atoms,
    received,
    target,
    kept,
    rest_hbm,
    edge_hbm,
    w_bil_hbm,
    w_up_hbm,
    w_atom_hbm,
    mid_hbm,
    *refs,
):
    *quarters, rest, edge_msg, w_bil_t, w_up, w_atom_in, edge_mid, message, sems = refs
    peers, half, lanes = received.shape
    width = w_bil_t.shape[0]
    pairs = [
        (rest_hbm, rest),
        (w_bil_hbm, w_bil_t),
        (w_up_hbm, w_up),
        (edge_hbm, edge_msg),
        (w_atom_hbm, w_atom_in),
    ]
    copies = [pltpu.make_async_copy(a, b, sems.at[i]) for i, (a, b) in enumerate(pairs)]
    start_first(copies)
    got = received[...].astype(F32).reshape(peers * half, lanes).T
    table = jnp.concatenate([got[:width], got[width:]], axis=1).astype(BF16)
    mixed = [dot_nt(table, kept[k]).astype(BF16) for k in range(kept.shape[0])]
    copies[0].wait()
    mixed += [dot_nt(table, rest[k]).astype(BF16) for k in range(rest.shape[0])]
    mixed = jnp.concatenate(mixed, axis=0)
    copies[1].wait()
    trip = silu(dot(w_bil_t[...], mixed)).T.astype(BF16)
    copies[2].wait()
    copies[3].wait()
    mid = (edge_msg[...].astype(F32) + dot(trip, w_up[...])).astype(BF16)
    edge_mid[...] = mid
    store = pltpu.make_async_copy(edge_mid, mid_hbm, sems.at[len(pairs)])
    store.start()
    local = target[...] - place("narrow", atoms)
    codes = [lax.shift_right_logical(local, 8), lax.bitwise_and(local, 255)]
    codes += [jnp.zeros_like(local)] * 14
    codes = jnp.concatenate(codes, axis=0).astype(F32).astype(BF16)
    copies[4].wait()
    message[...] = dot(mid, w_atom_in[...]).T.astype(BF16)
    part = message.shape[0] // len(quarters)
    mine = lax.axis_index("wide") % len(quarters)
    for q, quarter in enumerate(quarters):
        at = pl.multiple_of((mine ^ q) * part, part)
        quarter[:part, :] = message[pl.ds(at, part), :]
        quarter[part:, :] = codes
    store.wait()


def picks_kernel(order, feats, count, *refs):
    wanted = refs[:count]
    atom_h, gain, w_hbm = refs[count : count + 3]
    *given, gain_out, w_out, w, wide, tall, sem = refs[count + 3 :]
    fetch = pltpu.make_async_copy(w_hbm, w, sem)
    fetch.start()
    atoms = atom_h.shape[0]
    me = lax.axis_index("wide")
    starts = [pl.multiple_of(where(me) * feats, feats) for where in order]
    for i, want in enumerate(wanted):
        chosen = one_hot(want[...] - place("narrow", atoms), atoms)
        value = dot(chosen, atom_h[...]).astype(BF16)
        at = 0
        for hot, old in zip(given[2 * i :: 2 * count], given[2 * i + 1 :: 2 * count]):
            size = hot.shape[0]
            hot[...] = chosen[at : at + size]
            old[...] = value[at : at + size]
            at += size
    tall[...] = jnp.broadcast_to(gain[...], (tall.shape[1], gain.shape[1])).T
    blocks = [tall[pl.ds(at, feats), :] for at in starts]
    gain_out[...] = jnp.concatenate(blocks, axis=0).T[:8]
    fetch.wait()
    wide[...] = w[...].astype(F32)
    blocks = [wide[pl.ds(at, feats), :] for at in starts]
    w_out[...] = jnp.concatenate(blocks, axis=0).astype(BF16)


def sum_kernel(count, later, *refs):
    quarters, outs, total = refs[:count], refs[count + later : -1], refs[-1]
    me = lax.axis_index("wide")
    part, atoms = total.shape
    ids = iota((atoms, quarters[0].shape[1]), 0).astype(F32)
    value = jnp.zeros(total.shape, F32)
    for quarter in quarters:
        codes = quarter[part:, :].astype(F32)
        hot = jnp.where(ids == codes[0:1] * 256.0 + codes[1:2], 1.0, 0.0)
        value += dot_nt(quarter[:part, :], hot.astype(BF16))
    total[...] = value
    feats = total.shape[0] // len(outs)
    for i, out in enumerate(outs):
        k = -i % len(outs)
        at = pl.multiple_of((me // count ^ k) * feats, feats)
        out[...] = total[pl.ds(at, feats), :].astype(out.dtype)


def add_kernel(count, *refs):
    value = refs[0][...]
    for r in refs[1:count]:
        value = value + r[...].astype(F32)
    refs[-1][...] = value.astype(BF16)


def stacked(pieces):
    return jnp.concatenate([p[...] for p in pieces], axis=0)


def updated(hot, table, gain, w_atom, old):
    rows = dot_nt(hot, table)
    scale = lax.rsqrt(jnp.mean(rows * rows, axis=-1, keepdims=True) + 1e-06)
    normed = (rows * scale * gain).astype(BF16)
    return (old.astype(F32) + silu(dot(normed, w_atom))).astype(BF16)


def asked_kernel(count, *refs):
    sent = refs[len(refs) - count :]
    hots, olds = refs[: 2 * count : 2], refs[1 : 2 * count : 2]
    gain, w_atom = refs[2 * count : 2 * count + 2]
    table = stacked(refs[2 * count + 2 : len(refs) - count])
    for hot, old, send in zip(hots, olds, sent):
        send[...] = updated(hot[...], table, gain[:1, :], w_atom[...], old[...])


def local_kernel(gain, w_atom, atom_h, source, target, w_src, w_tgt, *refs):
    *pieces, atom_hbm, out, atom_out, sem = refs
    atoms = atom_h.shape[0]
    first = place("narrow", atoms)
    same = iota((atoms, atoms), 0) == iota((atoms, atoms), 1)
    same = jnp.where(same, 1.0, 0.0).astype(BF16)
    rows = updated(same, stacked(pieces), gain[:1, :], w_atom[...], atom_h[...])
    atom_out[...] = rows
    store = pltpu.make_async_copy(atom_out, atom_hbm, sem)
    store.start()
    sources = dot(one_hot(source[...] - first, atoms), rows).astype(BF16)
    targets = dot(one_hot(target[...] - first, atoms), rows).astype(BF16)
    out[...] = dot(sources, w_src[...]) + dot(targets, w_tgt[...])
    store.wait()


def final_kernel(count, start, *refs):
    partial, mid, w_src = refs[:3]
    rows = refs[3 : 3 + count]
    out_hbm, out, sems = refs[-3:]
    size = out.shape[0]
    these = slice(start, start + size)
    got = rows[0][...].astype(F32)
    for r in rows[1:]:
        got = got + r[...].astype(F32)
    got = got.astype(BF16)
    chunks = sems.shape[0]
    step = out.shape[1] // chunks
    stores = []
    for c in range(chunks):
        part = slice(c * step, (c + 1) * step)
        update = partial[these, part] + dot(got, w_src[:, part])
        out[:, part] = (mid[these, part].astype(F32) + silu(update)).astype(BF16)
        at = pl.ds(c * step, step)
        to = out_hbm.at[pl.ds(start, size), at]
        stores.append(pltpu.make_async_copy(out.at[:, at], to, sems.at[c]))
        stores[-1].start()
    for store in stores:
        store.wait()


def stage_factors(wide):
    stages = []
    left = wide
    size = min(4, max(1, wide // 4))
    stride = wide
    for f in (size, max(1, wide // (2 * size)), 2):
        if f > 1 and left % f == 0:
            stride //= f
            left //= f
            stages.append((stride, f))
    return stages


def gathered(share, wide, feats):
    groups = [(share, [lambda me: me])]
    stages = stage_factors(wide)
    for number, (stride, size) in enumerate(stages):
        mirror = size & (size - 1) == 0

        def turned(at, k, size=size, mirror=mirror):
            return at ^ k if mirror else (at + k) % size

        def moved(k, stride=stride, size=size, turned=turned, mirror=mirror):
            def owner(me):
                at = (me // stride) % size
                return me + (turned(at, k if mirror else size - k) - at) * stride
            return owner

        fresh = []
        for value, owners in groups:
            got = [(value, owners)]
            for k in range(1, size):
                pairs = []
                for i in range(wide):
                    at = (i // stride) % size
                    pairs.append((i, i + (turned(at, k) - at) * stride))
                back = moved(k)
                got.append(
                    (
                        value if value is None else lax.ppermute(value, "wide", pairs),
                        [lambda me, o=o, back=back: o(back(me)) for o in owners],
                    )
                )
            if size > 2:
                ranked = [got[0]] + got[:0:-1]
                for part in (ranked[: size // 2], ranked[size // 2 :]):
                    values = [v for v, _ in part]
                    fresh.append(
                        (
                            None if value is None else jnp.concatenate(values, axis=0),
                            [o for _, os in part for o in os],
                        )
                    )
            else:
                fresh.extend(got)
        groups = fresh
    return groups


def per_device(
    wide,
    narrow,
    edge_msg,
    basis,
    atom_h,
    edge_source,
    edge_target,
    send_rows,
    trip_slot,
    w_down,
    w_bil,
    w_up,
    w_atom_in,
    atom_gain,
    w_atom,
    w_src,
    w_tgt,
):
    edges, de = edge_msg.shape
    width = w_down.shape[1]
    basis_count = w_bil.shape[0] // width
    triplets = trip_slot.shape[1]
    atoms, da = atom_h.shape
    slots = send_rows.shape[1]
    cap = slots // wide
    feats = da // wide
    lanes = 2 * width
    bounds = [0, edges // 2, edges]
    sizes = [b - a for a, b in zip(bounds, bounds[1:])]
    low = min(4, wide)
    high = wide // low
    big = (24 << 20) if slots <= 512 else (60 << 20)
    shape = jax.ShapeDtypeStruct

    source = edge_source.reshape(1, edges)
    target = edge_target.reshape(1, edges)
    dma = pltpu.SemaphoreType.DMA

    outgoing, basis_near, slots_near = call(
        outgoing_kernel,
        [HBM] * 5,
        [VMEM] * 3,
        [
            shape((wide, cap // 2, lanes), BF16),
            shape(basis.shape, BF16),
            shape((triplets, edges), jnp.int32),
        ],
        big,
        scratch=[
            pltpu.VMEM((edges, de), BF16),
            pltpu.VMEM((width, de), BF16),
            pltpu.VMEM((1, slots), jnp.int32),
            dma((6,)),
        ],
        name="outgoing",
    )(edge_msg, w_down.T, send_rows, basis, trip_slot.T)
    received = lax.all_to_all(outgoing, "wide", split_axis=0, concat_axis=0, tiled=True)

    per = 256 // triplets
    kept = max(1, min(basis_count - 1, (3 << 20) // (edges * slots * 2)))
    rest_shape = (basis_count - kept, edges, slots)
    mixer = call(
        functools.partial(mixer_kernel, cap),
        [VMEM, VMEM],
        [VMEM, HBM],
        [shape((kept, edges, slots), BF16), shape(rest_shape, BF16)],
        big,
        scratch=[
            pltpu.VMEM((edges // per, per * triplets), jnp.int32),
            pltpu.VMEM(basis.shape, F32),
            pltpu.VMEM(rest_shape, BF16),
            dma((4,)),
        ],
        cost=cost(2 * basis_count * edges * slots * 256, 6 << 20),
        name="mixer",
    )(basis_near, slots_near)

    edge_mid, *quarters = call(
        functools.partial(edge_kernel, atoms),
        [VMEM] * 3 + [HBM] * 5,
        [HBM] + [VMEM] * low,
        [shape((edges, de), BF16)] + [shape((feats * high + 16, edges), BF16)] * low,
        big,
        scratch=[
            pltpu.VMEM(rest_shape, BF16),
            pltpu.VMEM((edges, de), BF16),
            pltpu.VMEM((width, basis_count * width), BF16),
            pltpu.VMEM(w_up.shape, BF16),
            pltpu.VMEM(w_atom_in.shape, BF16),
            pltpu.VMEM((edges, de), BF16),
            pltpu.VMEM((da, edges), BF16),
            dma((6,)),
        ],
        name="edge",
    )(received, target, *mixer, edge_msg, w_bil.T, w_up, w_atom_in)
    def mirrored(value, flip):
        return lax.ppermute(value, "wide", [(i, i ^ flip) for i in range(wide)])

    quarters = quarters[:1] + [mirrored(v, q) for q, v in enumerate(quarters) if q]
    source_late, quarters[1] = lax.optimization_barrier((source, quarters[1]))
    wanted = [
        lax.ppermute(source_late, "narrow", [(i, (i + k) % narrow) for i in range(narrow)])
        for k in range(1, narrow)
    ]
    def block(owner):
        return lambda me: owner(me) % low * high + owner(me) // low

    order = [block(o) for _, os in gathered(None, wide, feats) for o in os]
    *picks, gain_near, w_atom_near = call(
        functools.partial(picks_kernel, order, feats, len(wanted)),
        [VMEM] * (len(wanted) + 2) + [HBM],
        [VMEM] * (2 * len(sizes) * len(wanted) + 2),
        [shape((n, w), BF16) for n in sizes for _ in wanted for w in (atoms, da)]
        + [shape((8, da), F32), shape(w_atom.shape, BF16)],
        big,
        scratch=[
            pltpu.VMEM(w_atom.shape, BF16),
            pltpu.VMEM(w_atom.shape, F32),
            pltpu.VMEM((da, 128), F32),
            dma,
        ],
        cost=cost(1 << 26, 2 << 20),
        name="picks",
    )(*wanted, atom_h, atom_gain.reshape(1, da), w_atom)
    sums = call(
        functools.partial(sum_kernel, low, len(wanted)),
        [VMEM] * low + [pl.BlockSpec(memory_space=pl.ANY)] * len(wanted),
        [VMEM] * high,
        [shape((feats, atoms), F32)] + [shape((feats, atoms), BF16)] * (high - 1),
        big,
        scratch=[pltpu.VMEM((feats * high, atoms), F32)],
        name="sums",
    )(*quarters, *wanted)
    sums = [sums[0]] + [mirrored(v, -i % high * low) for i, v in enumerate(sums) if i]
    share = call(
        functools.partial(add_kernel, high),
        [VMEM] * high + [pl.BlockSpec(memory_space=pl.ANY)] * len(picks),
        VMEM,
        shape((feats, atoms), BF16),
        big,
        name="add",
    )(*sums, *picks)

    pieces = [v for v, _ in gathered(share, wide, feats)]
    rows = []
    for h, size in enumerate(sizes):
        given = picks[2 * len(wanted) * h : 2 * len(wanted) * (h + 1)]
        asked = call(
            functools.partial(asked_kernel, len(wanted)),
            [VMEM] * (len(given) + 2 + len(pieces)),
            [VMEM] * len(wanted),
            [shape((size, da), BF16)] * len(wanted),
            big,
            name=f"asked{h}",
        )(*given, gain_near, w_atom_near, *pieces)
        rows.append(
            [
                lax.ppermute(a, "narrow", [(i, (i - k) % narrow) for i in range(narrow)])
                for k, a in enumerate(asked, start=1)
            ]
        )
    atom_out, partial = call(
        local_kernel,
        [VMEM] * (7 + len(pieces)),
        [HBM, VMEM],
        (shape((atoms, da), BF16), shape((edges, de), F32)),
        big,
        scratch=[pltpu.VMEM((atoms, da), BF16), dma],
        cost=cost(4 * edges * da * de + 8 * edges * da * atoms, 4 << 20),
        name="local",
    )(gain_near, w_atom_near, atom_h, source, target, w_src, w_tgt, *pieces)
    edge_out = []
    for h, got in enumerate(rows):
        held = 3 + len(got) + len(edge_out)
        edge_out = [
            call(
                functools.partial(final_kernel, len(got), bounds[h]),
                [VMEM] * (3 + len(got)) + [HBM] * len(edge_out),
                HBM,
                shape((edges, de), BF16),
                big,
                scratch=[pltpu.VMEM((sizes[h], de), BF16), dma((2,))],
                name=f"final{h}",
                alias={held - 1: 0} if edge_out else {},
            )(partial, edge_mid, w_src, *got, *edge_out)
        ]
    edge_out = edge_out[0]
    return (edge_out, atom_out)


def solution(mesh):
    placed = (
        P(("wide", "narrow"), None),
        P(("wide", "narrow"), None),
        P("narrow", None),
        P(("wide", "narrow")),
        P(("wide", "narrow")),
        P(("wide", "narrow"), None),
        P(("wide", "narrow"), None),
        P(),
        P(),
        P(),
        P(),
        P(),
        P(),
        P(),
        P(),
    )
    return jax.shard_map(
        functools.partial(per_device, mesh.shape["wide"], mesh.shape["narrow"]),
        mesh=mesh,
        in_specs=placed,
        out_specs=(P(("wide", "narrow"), None), P("narrow", None)),
        check_vma=False,
    )
```

```python
import functools

import jax
import jax.numpy as jnp
from jax import lax
from jax.experimental import pallas as pl
from jax.experimental.pallas import tpu as pltpu
from jax.sharding import PartitionSpec as P

F32 = jnp.float32
BF16 = jnp.bfloat16
NT = (((1,), (1,)), ((), ()))


def silu(value):
    return value / (1.0 + jnp.exp(-value))


def dot(a, b):
    return jnp.dot(a, b, preferred_element_type=F32)


def dot_nt(a, b):
    return lax.dot_general(a, b, NT, preferred_element_type=F32)


def iota(shape, dim):
    return lax.broadcasted_iota(jnp.int32, shape, dim)


def column(row):
    return jnp.broadcast_to(row, (8, row.shape[1])).T[:, :1]


VMEM = pl.BlockSpec(memory_space=pltpu.VMEM)
HBM = pl.BlockSpec(memory_space=pltpu.HBM)


def quotient(value, by):
    if by & (by - 1) == 0:
        return lax.shift_right_logical(value, by.bit_length() - 1)
    return lax.div(value, jnp.int32(by))


def remainder(value, by):
    if by & (by - 1) == 0:
        return lax.bitwise_and(value, by - 1)
    return lax.rem(value, jnp.int32(by))


def call(kernel, ins, outs, out_shape, vmem, scratch=(), cost=None, name=None, alias=()):
    def kept(spec, leaf):
        return pltpu.HBM(leaf.shape, leaf.dtype) if spec is HBM else leaf

    many = isinstance(out_shape, (list, tuple))
    out_shape = [kept(o, s) for o, s in zip(outs, out_shape)] if many else kept(outs, out_shape)
    run = pl.pallas_call(
        kernel,
        out_shape=out_shape,
        in_specs=list(ins),
        out_specs=outs,
        scratch_shapes=list(scratch),
        input_output_aliases=dict(alias),
        compiler_params=pltpu.CompilerParams(vmem_limit_bytes=vmem),
        cost_estimate=cost,
        name=name,
    )

    def apply(*args):
        held = [
            pltpu.with_memory_space_constraint(a, pltpu.HBM) if spec is HBM else a
            for spec, a in zip(ins, args)
        ]
        return run(*held)

    return apply


def cost(flops, moved):
    return pl.CostEstimate(flops=int(flops), bytes_accessed=int(moved), transcendentals=0)


def place(axis, size):
    return lax.axis_index(axis) * size


def one_hot(index, count):
    hot = column(index) == iota((index.shape[1], count), 1)
    return jnp.where(hot, 1.0, 0.0).astype(BF16)


def outgoing_kernel(
    edge_hbm,
    w_hbm,
    rows_hbm,
    basis_hbm,
    slots_hbm,
    out,
    basis,
    slots_t,
    edge,
    w,
    rows,
    sems,
):
    edges = edge.shape[0]
    width = w.shape[0]
    peers, half, lanes = out.shape
    slots = peers * half * 2
    chunks = sems.shape[0] - 4
    step = edges // chunks
    copies = [
        pltpu.make_async_copy(rows_hbm, rows, sems.at[0]),
        pltpu.make_async_copy(w_hbm, w, sems.at[1]),
    ]
    for i in range(chunks):
        part = pl.ds(i * step, step)
        copies.append(pltpu.make_async_copy(edge_hbm.at[part, :], edge.at[part, :], sems.at[2 + i]))
    extra = [
        pltpu.make_async_copy(slots_hbm, slots_t, sems.at[2 + chunks]),
        pltpu.make_async_copy(basis_hbm, basis, sems.at[3 + chunks]),
    ]
    for c in copies + extra:
        c.start()
    copies[0].wait()
    hot = one_hot(rows[...], edges)
    copies[1].wait()
    down_w = w[...]
    twice = jnp.concatenate([down_w, down_w], axis=0)
    down = []
    for i in range(chunks):
        copies[2 + i].wait()
        down.append(silu(dot_nt(edge[i * step : (i + 1) * step, :], twice)).astype(BF16))
    picked = dot(hot, jnp.concatenate(down, axis=0))
    picked = picked.reshape(peers, 2 * half, lanes)
    low = iota((peers, half, lanes), 2) < width
    packed = jnp.where(low, picked[:, :half], picked[:, half:])
    out[...] = packed.astype(BF16)
    for c in extra:
        c.wait()


def start_first(copies):
    def go(_, carry):
        for c in copies:
            c.start()
        return carry

    lax.fori_loop(0, jnp.minimum(lax.axis_index("wide"), 0) + 1, go, 0)


def mixer_kernel(
    cap, basis, slots_t, kept, rest_hbm, flat, spread, rest, sems
):
    kept_count, edges, slots = kept.shape
    basis_count = kept_count + rest_hbm.shape[0]
    triplets = slots_t.shape[0]
    groups, span = flat.shape
    per = edges // groups
    total = basis.shape[1]
    rows, cols = iota((total, total), 0), iota((total, total), 1)
    order = quotient(rows, basis_count) + remainder(rows, basis_count) * triplets == cols
    order = jnp.where(order, 1.0, 0.0).astype(BF16)
    own = remainder(iota((edges, span), 0), per) == quotient(iota((edges, span), 1), triplets)
    half = cap // 2
    slot = slots_t[...]
    slot = (
        remainder(quotient(slot, half), 2) * (slots // 2)
        + quotient(slot, cap) * half
        + remainder(slot, half)
    )
    slot = slot.T
    turn = remainder(iota((triplets, span), 1), triplets)
    tile = jnp.where(iota((triplets, span), 0) == turn, 1.0, 0.0)
    tile = tile.astype(BF16)
    high = lax.shift_right_logical(slot, 8).astype(F32).astype(BF16)
    low = lax.bitwise_and(slot, 255).astype(F32).astype(BF16)
    wide = jnp.where(own, dot(high, tile) * 256.0 + dot(low, tile), 0.0)
    flat[...] = jnp.sum(wide.reshape(groups, per, span), axis=1).astype(jnp.int32)
    by_basis = dot(basis[...], order)
    pack = 128 // triplets
    turn = remainder(iota((edges, 128), 0), pack)
    for q in range(total // 128):
        lanes = by_basis[:, q * 128 : (q + 1) * 128]
        turned = lanes
        for r in range(1, pack):
            turned = jnp.where(turn == r, pltpu.roll(lanes, r * triplets, 1), turned)
        spread[:, q * 128 : (q + 1) * 128] = turned
    row, lane = iota((per, 128), 0), quotient(iota((per, 128), 1), triplets)
    mine = [row == lane + c * pack for c in range(span // 128)]

    def one(pair):
        parts = []
        for h in range(2):
            group = pair * 2 + h
            values = spread[pl.ds(pl.multiple_of(group * per, per), per), :]
            left = []
            for k in range(basis_count):
                q, j = k // pack, k % pack
                lanes = values[:, q * 128 : (q + 1) * 128]
                if j:
                    lanes = pltpu.roll(lanes, 128 - j * triplets, 1)
                left.append(jnp.concatenate([jnp.where(m, lanes, 0.0) for m in mine], axis=1))
            left = jnp.concatenate(left, axis=0).astype(BF16)
            hot = iota((slots, span), 0) == flat[pl.ds(group, 1), :]
            part = dot_nt(left, jnp.where(hot, 1.0, 0.0).astype(BF16))
            parts.append(part.reshape(basis_count, per, slots))
        both = jnp.concatenate(parts, axis=1).astype(BF16)
        at = pl.ds(pl.multiple_of(pair * 2 * per, 2 * per), 2 * per)
        kept[:, at, :] = both[:kept_count]
        rest[:, at, :] = both[kept_count:]

    unroll = 4

    def step(i, _):
        for u in range(unroll):
            one(unroll * i + u)
        return 0

    chunks = sems.shape[0]
    steps = groups // 2 // unroll // chunks
    copies = []
    for c in range(chunks):
        lax.fori_loop(c * steps, (c + 1) * steps, step, 0)
        size = steps * unroll * 2 * per
        part = pl.ds(c * size, size)
        copies.append(
            pltpu.make_async_copy(rest.at[:, part, :], rest_hbm.at[:, part, :], sems.at[c])
        )
        copies[-1].start()
    for c in copies:
        c.wait()


def edge_kernel(
    atoms,
    received,
    target,
    kept,
    rest_hbm,
    edge_hbm,
    w_bil_hbm,
    w_up_hbm,
    w_atom_hbm,
    mid_hbm,
    *refs,
):
    *quarters, rest, edge_msg, w_bil_t, w_up, w_atom_in, edge_mid, message, sems = refs
    peers, half, lanes = received.shape
    width = w_bil_t.shape[0]
    pairs = [
        (rest_hbm, rest),
        (w_bil_hbm, w_bil_t),
        (w_up_hbm, w_up),
        (edge_hbm, edge_msg),
        (w_atom_hbm, w_atom_in),
    ]
    copies = [pltpu.make_async_copy(a, b, sems.at[i]) for i, (a, b) in enumerate(pairs)]
    start_first(copies)
    got = received[...].astype(F32).reshape(peers * half, lanes).T
    table = jnp.concatenate([got[:width], got[width:]], axis=1).astype(BF16)
    mixed = [dot_nt(table, kept[k]).astype(BF16) for k in range(kept.shape[0])]
    copies[0].wait()
    mixed += [dot_nt(table, rest[k]).astype(BF16) for k in range(rest.shape[0])]
    mixed = jnp.concatenate(mixed, axis=0)
    copies[1].wait()
    trip = silu(dot(w_bil_t[...], mixed)).T.astype(BF16)
    copies[2].wait()
    copies[3].wait()
    mid = (edge_msg[...].astype(F32) + dot(trip, w_up[...])).astype(BF16)
    edge_mid[...] = mid
    store = pltpu.make_async_copy(edge_mid, mid_hbm, sems.at[len(pairs)])
    store.start()
    local = target[...] - place("narrow", atoms)
    codes = [lax.shift_right_logical(local, 8), lax.bitwise_and(local, 255)]
    codes += [jnp.zeros_like(local)] * 14
    codes = jnp.concatenate(codes, axis=0).astype(F32).astype(BF16)
    copies[4].wait()
    message[...] = dot(mid, w_atom_in[...]).T.astype(BF16)
    part = message.shape[0] // len(quarters)
    mine = lax.axis_index("wide") % len(quarters)
    for q, quarter in enumerate(quarters):
        at = pl.multiple_of((mine ^ q) * part, part)
        quarter[:part, :] = message[pl.ds(at, part), :]
        quarter[part:, :] = codes
    store.wait()


def picks_kernel(order, feats, count, *refs):
    wanted = refs[:count]
    atom_h, gain, w_hbm = refs[count : count + 3]
    *given, gain_out, w_out, w, wide, tall, sem = refs[count + 3 :]
    fetch = pltpu.make_async_copy(w_hbm, w, sem)
    fetch.start()
    atoms = atom_h.shape[0]
    me = lax.axis_index("wide")
    starts = [pl.multiple_of(where(me) * feats, feats) for where in order]
    for i, want in enumerate(wanted):
        chosen = one_hot(want[...] - place("narrow", atoms), atoms)
        value = dot(chosen, atom_h[...]).astype(BF16)
        at = 0
        for hot, old in zip(given[2 * i :: 2 * count], given[2 * i + 1 :: 2 * count]):
            size = hot.shape[0]
            hot[...] = chosen[at : at + size]
            old[...] = value[at : at + size]
            at += size
    tall[...] = jnp.broadcast_to(gain[...], (tall.shape[1], gain.shape[1])).T
    blocks = [tall[pl.ds(at, feats), :] for at in starts]
    gain_out[...] = jnp.concatenate(blocks, axis=0).T[:8]
    fetch.wait()
    wide[...] = w[...].astype(F32)
    blocks = [wide[pl.ds(at, feats), :] for at in starts]
    w_out[...] = jnp.concatenate(blocks, axis=0).astype(BF16)


def sum_kernel(count, later, *refs):
    quarters, outs, total = refs[:count], refs[count + later : -1], refs[-1]
    me = lax.axis_index("wide")
    part, atoms = total.shape
    ids = iota((atoms, quarters[0].shape[1]), 0).astype(F32)
    value = jnp.zeros(total.shape, F32)
    for quarter in quarters:
        codes = quarter[part:, :].astype(F32)
        hot = jnp.where(ids == codes[0:1] * 256.0 + codes[1:2], 1.0, 0.0)
        value += dot_nt(quarter[:part, :], hot.astype(BF16))
    total[...] = value
    feats = total.shape[0] // len(outs)
    for i, out in enumerate(outs):
        k = -i % len(outs)
        at = pl.multiple_of((me // count ^ k) * feats, feats)
        out[...] = total[pl.ds(at, feats), :].astype(out.dtype)


def add_kernel(count, *refs):
    value = refs[0][...]
    for r in refs[1:count]:
        value = value + r[...].astype(F32)
    refs[-1][...] = value.astype(BF16)


def stacked(pieces):
    return jnp.concatenate([p[...] for p in pieces], axis=0)


def updated(hot, table, gain, w_atom, old):
    rows = dot_nt(hot, table)
    scale = lax.rsqrt(jnp.mean(rows * rows, axis=-1, keepdims=True) + 1e-06)
    normed = (rows * scale * gain).astype(BF16)
    return (old.astype(F32) + silu(dot(normed, w_atom))).astype(BF16)


def asked_kernel(count, *refs):
    sent = refs[len(refs) - count :]
    hots, olds = refs[: 2 * count : 2], refs[1 : 2 * count : 2]
    gain, w_atom = refs[2 * count : 2 * count + 2]
    table = stacked(refs[2 * count + 2 : len(refs) - count])
    for hot, old, send in zip(hots, olds, sent):
        send[...] = updated(hot[...], table, gain[:1, :], w_atom[...], old[...])


def local_kernel(gain, w_atom, atom_h, source, target, w_src, w_tgt, *refs):
    *pieces, atom_hbm, out, atom_out, sem = refs
    atoms = atom_h.shape[0]
    first = place("narrow", atoms)
    same = iota((atoms, atoms), 0) == iota((atoms, atoms), 1)
    same = jnp.where(same, 1.0, 0.0).astype(BF16)
    rows = updated(same, stacked(pieces), gain[:1, :], w_atom[...], atom_h[...])
    atom_out[...] = rows
    store = pltpu.make_async_copy(atom_out, atom_hbm, sem)
    store.start()
    sources = dot(one_hot(source[...] - first, atoms), rows).astype(BF16)
    targets = dot(one_hot(target[...] - first, atoms), rows).astype(BF16)
    out[...] = dot(sources, w_src[...]) + dot(targets, w_tgt[...])
    store.wait()


def final_kernel(count, start, *refs):
    partial, mid, w_src = refs[:3]
    rows = refs[3 : 3 + count]
    out_hbm, out, sems = refs[-3:]
    size = out.shape[0]
    these = slice(start, start + size)
    got = rows[0][...].astype(F32)
    for r in rows[1:]:
        got = got + r[...].astype(F32)
    got = got.astype(BF16)
    chunks = sems.shape[0]
    step = out.shape[1] // chunks
    stores = []
    for c in range(chunks):
        part = slice(c * step, (c + 1) * step)
        update = partial[these, part] + dot(got, w_src[:, part])
        out[:, part] = (mid[these, part].astype(F32) + silu(update)).astype(BF16)
        at = pl.ds(c * step, step)
        to = out_hbm.at[pl.ds(start, size), at]
        stores.append(pltpu.make_async_copy(out.at[:, at], to, sems.at[c]))
        stores[-1].start()
    for store in stores:
        store.wait()


def stage_factors(wide):
    stages = []
    left = wide
    size = min(4, max(1, wide // 4))
    stride = wide
    for f in (size, max(1, wide // (2 * size)), 2):
        if f > 1 and left % f == 0:
            stride //= f
            left //= f
            stages.append((stride, f))
    return stages


def gathered(share, wide, feats):
    groups = [(share, [lambda me: me])]
    stages = stage_factors(wide)
    for number, (stride, size) in enumerate(stages):
        mirror = size & (size - 1) == 0

        def turned(at, k, size=size, mirror=mirror):
            return at ^ k if mirror else (at + k) % size

        def moved(k, stride=stride, size=size, turned=turned, mirror=mirror):
            def owner(me):
                at = (me // stride) % size
                return me + (turned(at, k if mirror else size - k) - at) * stride
            return owner

        fresh = []
        for value, owners in groups:
            got = [(value, owners)]
            for k in range(1, size):
                pairs = []
                for i in range(wide):
                    at = (i // stride) % size
                    pairs.append((i, i + (turned(at, k) - at) * stride))
                back = moved(k)
                got.append(
                    (
                        value if value is None else lax.ppermute(value, "wide", pairs),
                        [lambda me, o=o, back=back: o(back(me)) for o in owners],
                    )
                )
            if size > 2:
                ranked = [got[0]] + got[:0:-1]
                for part in (ranked[: size // 2], ranked[size // 2 :]):
                    values = [v for v, _ in part]
                    fresh.append(
                        (
                            None if value is None else jnp.concatenate(values, axis=0),
                            [o for _, os in part for o in os],
                        )
                    )
            else:
                fresh.extend(got)
        groups = fresh
    return groups


def per_device(
    wide,
    narrow,
    edge_msg,
    basis,
    atom_h,
    edge_source,
    edge_target,
    send_rows,
    trip_slot,
    w_down,
    w_bil,
    w_up,
    w_atom_in,
    atom_gain,
    w_atom,
    w_src,
    w_tgt,
):
    edges, de = edge_msg.shape
    width = w_down.shape[1]
    basis_count = w_bil.shape[0] // width
    triplets = trip_slot.shape[1]
    atoms, da = atom_h.shape
    slots = send_rows.shape[1]
    cap = slots // wide
    feats = da // wide
    lanes = 2 * width
    bounds = [0, edges // 2, edges]
    sizes = [b - a for a, b in zip(bounds, bounds[1:])]
    low = min(4, wide)
    high = wide // low
    big = (24 << 20) if slots <= 512 else (60 << 20)
    shape = jax.ShapeDtypeStruct

    source = edge_source.reshape(1, edges)
    target = edge_target.reshape(1, edges)
    dma = pltpu.SemaphoreType.DMA

    outgoing, basis_near, slots_near = call(
        outgoing_kernel,
        [HBM] * 5,
        [VMEM] * 3,
        [
            shape((wide, cap // 2, lanes), BF16),
            shape(basis.shape, BF16),
            shape((triplets, edges), jnp.int32),
        ],
        big,
        scratch=[
            pltpu.VMEM((edges, de), BF16),
            pltpu.VMEM((width, de), BF16),
            pltpu.VMEM((1, slots), jnp.int32),
            dma((5,)),
        ],
        name="outgoing",
    )(edge_msg, w_down.T, send_rows, basis, trip_slot.T)
    received = lax.all_to_all(outgoing, "wide", split_axis=0, concat_axis=0, tiled=True)

    per = 256 // triplets
    kept = max(1, min(basis_count - 1, (3 << 20) // (edges * slots * 2)))
    rest_shape = (basis_count - kept, edges, slots)
    mixer = call(
        functools.partial(mixer_kernel, cap),
        [VMEM, VMEM],
        [VMEM, HBM],
        [shape((kept, edges, slots), BF16), shape(rest_shape, BF16)],
        big,
        scratch=[
            pltpu.VMEM((edges // per, per * triplets), jnp.int32),
            pltpu.VMEM(basis.shape, F32),
            pltpu.VMEM(rest_shape, BF16),
            dma((4,)),
        ],
        cost=cost(2 * basis_count * edges * slots * 256, 6 << 20),
        name="mixer",
    )(basis_near, slots_near)

    edge_mid, *quarters = call(
        functools.partial(edge_kernel, atoms),
        [VMEM] * 3 + [HBM] * 5,
        [HBM] + [VMEM] * low,
        [shape((edges, de), BF16)] + [shape((feats * high + 16, edges), BF16)] * low,
        big,
        scratch=[
            pltpu.VMEM(rest_shape, BF16),
            pltpu.VMEM((edges, de), BF16),
            pltpu.VMEM((width, basis_count * width), BF16),
            pltpu.VMEM(w_up.shape, BF16),
            pltpu.VMEM(w_atom_in.shape, BF16),
            pltpu.VMEM((edges, de), BF16),
            pltpu.VMEM((da, edges), BF16),
            dma((6,)),
        ],
        name="edge",
    )(received, target, *mixer, edge_msg, w_bil.T, w_up, w_atom_in)
    def mirrored(value, flip):
        return lax.ppermute(value, "wide", [(i, i ^ flip) for i in range(wide)])

    quarters = quarters[:1] + [mirrored(v, q) for q, v in enumerate(quarters) if q]
    source_late, quarters[1] = lax.optimization_barrier((source, quarters[1]))
    wanted = [
        lax.ppermute(source_late, "narrow", [(i, (i + k) % narrow) for i in range(narrow)])
        for k in range(1, narrow)
    ]
    def block(owner):
        return lambda me: owner(me) % low * high + owner(me) // low

    order = [block(o) for _, os in gathered(None, wide, feats) for o in os]
    *picks, gain_near, w_atom_near = call(
        functools.partial(picks_kernel, order, feats, len(wanted)),
        [VMEM] * (len(wanted) + 2) + [HBM],
        [VMEM] * (2 * len(sizes) * len(wanted) + 2),
        [shape((n, w), BF16) for n in sizes for _ in wanted for w in (atoms, da)]
        + [shape((8, da), F32), shape(w_atom.shape, BF16)],
        big,
        scratch=[
            pltpu.VMEM(w_atom.shape, BF16),
            pltpu.VMEM(w_atom.shape, F32),
            pltpu.VMEM((da, 128), F32),
            dma,
        ],
        cost=cost(1 << 26, 2 << 20),
        name="picks",
    )(*wanted, atom_h, atom_gain.reshape(1, da), w_atom)
    sums = call(
        functools.partial(sum_kernel, low, len(wanted)),
        [VMEM] * low + [pl.BlockSpec(memory_space=pl.ANY)] * len(wanted),
        [VMEM] * high,
        [shape((feats, atoms), F32)] + [shape((feats, atoms), BF16)] * (high - 1),
        big,
        scratch=[pltpu.VMEM((feats * high, atoms), F32)],
        name="sums",
    )(*quarters, *wanted)
    sums = [sums[0]] + [mirrored(v, -i % high * low) for i, v in enumerate(sums) if i]
    share = call(
        functools.partial(add_kernel, high),
        [VMEM] * high + [pl.BlockSpec(memory_space=pl.ANY)] * len(picks),
        VMEM,
        shape((feats, atoms), BF16),
        big,
        name="add",
    )(*sums, *picks)

    pieces = [v for v, _ in gathered(share, wide, feats)]
    rows = []
    for h, size in enumerate(sizes):
        given = picks[2 * len(wanted) * h : 2 * len(wanted) * (h + 1)]
        asked = call(
            functools.partial(asked_kernel, len(wanted)),
            [VMEM] * (len(given) + 2 + len(pieces)),
            [VMEM] * len(wanted),
            [shape((size, da), BF16)] * len(wanted),
            big,
            name=f"asked{h}",
        )(*given, gain_near, w_atom_near, *pieces)
        rows.append(
            [
                lax.ppermute(a, "narrow", [(i, (i - k) % narrow) for i in range(narrow)])
                for k, a in enumerate(asked, start=1)
            ]
        )
    atom_out, partial = call(
        local_kernel,
        [VMEM] * (7 + len(pieces)),
        [HBM, VMEM],
        (shape((atoms, da), BF16), shape((edges, de), F32)),
        big,
        scratch=[pltpu.VMEM((atoms, da), BF16), dma],
        cost=cost(4 * edges * da * de + 8 * edges * da * atoms, 4 << 20),
        name="local",
    )(gain_near, w_atom_near, atom_h, source, target, w_src, w_tgt, *pieces)
    edge_out = []
    for h, got in enumerate(rows):
        held = 3 + len(got) + len(edge_out)
        edge_out = [
            call(
                functools.partial(final_kernel, len(got), bounds[h]),
                [VMEM] * (3 + len(got)) + [HBM] * len(edge_out),
                HBM,
                shape((edges, de), BF16),
                big,
                scratch=[pltpu.VMEM((sizes[h], de), BF16), dma((2,))],
                name=f"final{h}",
                alias={held - 1: 0} if edge_out else {},
            )(partial, edge_mid, w_src, *got, *edge_out)
        ]
    edge_out = edge_out[0]
    return (edge_out, atom_out)


def solution(mesh):
    placed = (
        P(("wide", "narrow"), None),
        P(("wide", "narrow"), None),
        P("narrow", None),
        P(("wide", "narrow")),
        P(("wide", "narrow")),
        P(("wide", "narrow"), None),
        P(("wide", "narrow"), None),
        P(),
        P(),
        P(),
        P(),
        P(),
        P(),
        P(),
        P(),
    )
    return jax.shard_map(
        functools.partial(per_device, mesh.shape["wide"], mesh.shape["narrow"]),
        mesh=mesh,
        in_specs=placed,
        out_specs=(P(("wide", "narrow"), None), P("narrow", None)),
        check_vma=False,
    )
```
